512 devices in a mesh: slot: 16 (over z_lo, x), row: 32 (over y, z_hi, core).
Axes of the slice: x: 4, y: 4, z: 16 (z_hi: 4, z_lo: 4; z = z_hi * 4 + z_lo), core: 2. Of those that a mesh axis runs over, the one named last changes fastest.
Arguments:
- drift: bfloat16 [2048, 2048], P(('slot', 'row')), may hold values from -1 to 1, as said below
- ctrl_blocks: bfloat16 [16, 128, 128], replicated, may hold values from -0.125 to 0.125
- blk_pos: int32 [16, 2], replicated, may hold values from 0 to 15
- amps: float32 [16, 16], P('slot'), may hold values from -4 to 4
- init_states: float32 [2, 512, 2048], P(None, 'row'), may hold values from -6 to 6
- targets: float32 [2, 512, 2048], P(None, 'row'), may hold values from -50 to 50
Outputs:
- states: float32 [16, 2, 512, 2048], P('slot', None, 'row')
- grads: float32 [16, 16], P('slot')
The draws below stay inside these ranges and needn't reach their ends.
Inputs may be any that keep to these rules, and one draw needn't show every extreme that they name: drift is symmetric.
All inputs are finite; a program needn't handle non-finite values.
Results may differ from the reference program's by a relative error of at most 0.038.
Values may be sent and summed in bfloat16 or wider, within the bound.
No kernel may reach another device: no remote copies, remote signals or barrier semaphores. Data moves between devices by JAX's collectives and lax.ppermute only.
A program may use at most 64 MiB of HBM per device.

```python
import math
import jax
import jax.numpy as jnp
from jax import lax

N = 2048
BLOCK = 128
CONTROLS = 16
TAYLOR = 4
COLS = 512
SLOTS = 16
NB = 16


def draw_drift(key, part):
    base = jnp.clip(jax.random.normal(key, (N, N), jnp.float32), -4.0, 4.0)
    symmetric = (base + base.T) * (0.70710678 * 0.9 / math.sqrt(N))
    return symmetric.astype(jnp.bfloat16)


def draw_targets(key, part):
    key_noise = jax.random.fold_in(key, 11)
    key_entry = jax.random.fold_in(key, 12)
    column = jnp.arange(COLS).astype(jnp.float32) / max(COLS - 1, 1)
    entry_scale = jnp.power(10.0, jax.random.uniform(key_entry, (N,), jnp.float32, 0.0, 1.0))
    noise = jnp.clip(jax.random.normal(key_noise, (2, COLS, N), jnp.float32), -4.0, 4.0)
    column_scale = jnp.power(10.0, column)
    return noise * column_scale[None, :, None] * entry_scale[None, None, :] * 0.1


def touch_ends(values, rng, least, largest):
    longest = values.shape.index(max(values.shape))
    spots = []
    for shift in (0, 1):
        where = [jax.random.randint(jax.random.fold_in(rng, axis), (), 0, length) for axis, length in enumerate(values.shape)]
        where[longest] = (where[longest] + shift) % values.shape[longest]
        spots.append(tuple(where))
    return values.at[spots[0]].set(least).at[spots[1]].set(largest)


def level_of(own_key, shape, cuts, low, largest):
    factor_of = 1.0
    for dim, shards_of in cuts:
        heights = jax.random.uniform(jax.random.fold_in(jax.random.fold_in(own_key, 6), dim), (shards_of,), jnp.float32, low / len(cuts), largest / len(cuts))
        factor_of = factor_of * jnp.repeat(jnp.exp(heights), shape[dim] // shards_of).reshape((-1,) + (1,) * (len(shape) - 1 - dim))
    return factor_of


def normal_values(key, shape, scale, reach, pieces=(), dtype=jnp.bfloat16):
    array = jax.random.normal(key, shape, jnp.float32) * scale
    if len(pieces) > 0:
        array = level_of(key, shape, pieces, -0.22, 0.18) * array
    return jnp.clip(array, min=-reach, max=reach).astype(dtype)


def setup_inputs(seed: int = 0) -> dict:
    splits = jax.random.split(jax.random.key(seed), 7)
    drift = draw_drift(jax.random.fold_in(splits[6], 71), 0)
    ctrl_blocks = normal_values(splits[1], (CONTROLS, BLOCK, BLOCK), (16 * BLOCK) ** -0.5, 0.125)
    blk_pos = touch_ends(jax.random.randint(splits[2], (CONTROLS, 2), 0, N // BLOCK), jax.random.fold_in(splits[2], 1), 0, (N // BLOCK) - 1).astype(jnp.int32)
    amps = normal_values(splits[3], (SLOTS, CONTROLS), 1.0, 4.0, ((0, 16),), jnp.float32)
    init_states = normal_values(splits[4], (2, COLS, N), 1.0, 6.0, ((1, 32),), jnp.float32)
    targets = draw_targets(jax.random.fold_in(splits[6], 71), 0)
    return {"drift": drift, "ctrl_blocks": ctrl_blocks, "blk_pos": blk_pos, "amps": amps, "init_states": init_states, "targets": targets}


def apply_hamiltonian(rounded, drift, ctrl_blocks, row_pick, col_pick, row_hot, col_hot, amps_row):
    halves, columns, extent = rounded.shape
    block_size = ctrl_blocks.shape[1]
    flat_rows = rounded.reshape(halves * columns, extent)
    drift_part = jnp.dot(flat_rows, drift, preferred_element_type=jnp.float32)
    tile_rows = flat_rows.reshape(halves * columns, extent // block_size, block_size)
    from_col = jnp.take(tile_rows, col_pick, axis=1).astype(jnp.float32)
    from_row = jnp.take(tile_rows, row_pick, axis=1).astype(jnp.float32)
    blocks = ctrl_blocks.astype(jnp.float32)
    upper_part = jnp.einsum("mkb,kab->mka", from_col, blocks) * amps_row[None, :, None]
    lower_part = jnp.einsum("mka,kab->mkb", from_row, blocks) * amps_row[None, :, None]
    placed = jnp.einsum("mka,kn->mna", upper_part, row_hot, precision=lax.Precision.HIGHEST)
    placed = placed + jnp.einsum("mkb,kn->mnb", lower_part, col_hot, precision=lax.Precision.HIGHEST)
    summed = drift_part + placed.reshape(halves * columns, extent)
    return summed.reshape(halves, columns, extent)


def propagate(state, forward, apply_fn):
    summed = state
    series_term = state
    for degree in range(1, TAYLOR + 1):
        applied = apply_fn(series_term.astype(jnp.bfloat16))
        if forward:
            turned = jnp.stack([applied[1], -applied[0]])
        else:
            turned = jnp.stack([-applied[1], applied[0]])
        series_term = turned * (1.0 / degree)
        summed = summed + series_term
    return summed


def control_grads(state, adjoint, ctrl_blocks, row_pick, col_pick, scale):
    halves, columns, extent = state.shape
    block_size = ctrl_blocks.shape[1]
    shape_tiles = (halves * columns, extent // block_size, block_size)
    source = jnp.stack([state[1].astype(jnp.bfloat16), -state[0].astype(jnp.bfloat16)]).reshape(shape_tiles)
    weights = adjoint.astype(jnp.bfloat16).reshape(shape_tiles)
    blocks = ctrl_blocks.astype(jnp.float32)
    upper_part = jnp.einsum("mkb,kab->mka", jnp.take(source, col_pick, axis=1).astype(jnp.float32), blocks)
    lower_part = jnp.einsum("mka,kab->mkb", jnp.take(source, row_pick, axis=1).astype(jnp.float32), blocks)
    inner_sum = jnp.sum(jnp.take(weights, row_pick, axis=1).astype(jnp.float32) * upper_part, axis=(0, 2))
    inner_sum = inner_sum + jnp.sum(jnp.take(weights, col_pick, axis=1).astype(jnp.float32) * lower_part, axis=(0, 2))
    return inner_sum * scale


def reference(drift, ctrl_blocks, blk_pos, amps, init_states, targets):
    row_pick = blk_pos[:, 0].astype(jnp.int32)
    col_pick = blk_pos[:, 1].astype(jnp.int32)
    positions = lax.broadcasted_iota(jnp.int32, (CONTROLS, NB), 1)
    row_hot = (positions == row_pick[:, None]).astype(jnp.float32)
    col_hot = (positions == col_pick[:, None]).astype(jnp.float32)

    def slot_apply(amps_row):
        return lambda rounded: apply_hamiltonian(rounded, drift, ctrl_blocks, row_pick, col_pick, row_hot, col_hot, amps_row)

    def forward_step(state, amps_row):
        result = propagate(state, True, slot_apply(amps_row))
        return result, result

    def adjoint_step(state, amps_row):
        result = propagate(state, False, slot_apply(amps_row))
        return result, result

    _, states = lax.scan(forward_step, init_states, amps)
    _, earlier = lax.scan(adjoint_step, targets, amps[1:], reverse=True)
    lams = jnp.concatenate([earlier, targets[None]], axis=0)
    scale = 1.0 / COLS

    def slot_grads(pair):
        return control_grads(pair[0], pair[1], ctrl_blocks, row_pick, col_pick, scale)

    grads = lax.map(slot_grads, (states, lams))
    return states, grads
```

```python
import jax
import jax.numpy as jnp
from jax import lax
from jax.experimental import pallas as pl
from jax.experimental.pallas import tpu as pltpu
from jax.sharding import PartitionSpec as P

ZL, X, Y, ZH, CORES = 4, 4, 4, 4, 2
BLOCK = 128
NB = 16
KEPT = NB // 2 + 1
PIECES = KEPT + 1
SLOTS = 16
CONTROLS = 16
BF = jnp.bfloat16


def source_of(index):
    r = index & 3
    zh = (index >> 2) & 3
    y = (index >> 4) & 3
    c = index >> 6
    return y * 32 + zh * 8 + c * 4 + r


def pick_matrix(dtype):
    rows = lax.broadcasted_iota(jnp.int32, (BLOCK, BLOCK), 0)
    cols = lax.broadcasted_iota(jnp.int32, (BLOCK, BLOCK), 1)
    return jnp.where(source_of(rows) == cols, 1.0, 0.0).astype(dtype)


def mm(a, b):
    return jnp.dot(a, b, preferred_element_type=jnp.float32)


def mm_t(a, b):
    return lax.dot_general(a, b, (((1,), (1,)), ((), ())), preferred_element_type=jnp.float32)


def at(start, size=BLOCK):
    return pl.ds(pl.multiple_of(start, size), size)


def chain_kernel(
    amps_ref, meta_ref, own_ref, other_ref, ctrl_ref, init_ref, target_ref, out_ref,
    even_h, odd_h, x_ref, pieces_ref, base_ref, work_ref,
):
    zl, xx = lax.axis_index("zl"), lax.axis_index("x")
    core = lax.axis_index("c")
    member = zl * X + xx
    backward = member >= SLOTS // 2
    lane = lax.rem(member, SLOTS // 2)
    pick = pick_matrix(BF)

    def lay(block_row, _):
        base = block_row * BLOCK
        zl_of = lax.div(block_row, X)
        x_of = lax.rem(block_row, X)
        for step in range(KEPT):
            col = lax.rem(block_row + step, NB) * BLOCK
            for ref, half in ((own_ref, core), (other_ref, 1 - core)):
                tiles = [ref[x_of * Y + y, zl_of * PIECES + step] for y in range(Y)]
                rows = pl.ds(pl.multiple_of(base + half * 64, 64), 64)
                even_h[rows, at(col)] = jnp.concatenate(tiles, axis=0)
        return 0

    lax.fori_loop(0, NB, lay, 0)
    eye = jnp.where(
        lax.broadcasted_iota(jnp.int32, (BLOCK, BLOCK), 0)
        == lax.broadcasted_iota(jnp.int32, (BLOCK, BLOCK), 1),
        1.0,
        0.0,
    ).astype(BF)

    def mirror(block_row, _):
        for step in range(1, NB // 2):
            other_row = lax.rem(block_row + step, NB) * BLOCK
            turned = mm_t(eye, even_h[at(block_row * BLOCK), at(other_row)])
            even_h[at(other_row), at(block_row * BLOCK)] = turned.astype(BF)
        return 0

    lax.fori_loop(0, NB, mirror, 0)

    def copy(block_row, _):
        odd_h[at(block_row * BLOCK), :] = even_h[at(block_row * BLOCK), :]
        return 0

    lax.fori_loop(0, NB, copy, 0)

    for k in range(CONTROLS):
        turned = mm(pick, ctrl_ref[k]).astype(BF)
        pieces_ref[k] = mm_t(turned, pick).astype(BF)
        pieces_ref[CONTROLS + k] = mm_t(pick, turned).astype(BF)

    def gather_base(p, _):
        base_ref[p] = even_h[at(meta_ref[0, p]), at(meta_ref[1, p])].astype(jnp.float32)
        return 0

    lax.fori_loop(0, 2 * CONTROLS, gather_base, 0)

    def scaled(p, slot):
        lead = meta_ref[2, p]
        start = jnp.where(lead == p, base_ref[p], work_ref[lead])
        amp = amps_ref[slot, p % CONTROLS]
        work_ref[lead] = start + amp * pieces_ref[p].astype(jnp.float32)

    def placed(p, target):
        value = work_ref[meta_ref[2, p]].astype(BF)
        target[at(meta_ref[0, p]), at(meta_ref[1, p])] = value

    def slot_of(step):
        return jnp.where(backward, SLOTS - 1 - step, step)

    def build(step, target):
        slot = slot_of(jnp.minimum(step, SLOTS - 1))
        for p in range(2 * CONTROLS):
            scaled(p, slot)
        for p in range(2 * CONTROLS):
            placed(p, target)

    x_ref[...] = jnp.zeros_like(x_ref)

    def load_from(ref):
        for part in range(2):
            for half in range(2):
                row = part * 4 + half
                x_ref[row : row + 1, :] = ref[part, pl.ds(lane + half * 8, 1), :]

    @pl.when(backward)
    def _():
        load_from(target_ref)

    @pl.when(jnp.logical_not(backward))
    def _():
        load_from(init_ref)

    for block in range(NB):
        cols = slice(block * BLOCK, (block + 1) * BLOCK)
        value = x_ref[:, cols]
        high = value.astype(BF)
        rest = value - high.astype(jnp.float32)
        middle = rest.astype(BF)
        low = (rest - middle.astype(jnp.float32)).astype(BF)
        x_ref[:, cols] = mm_t(high, pick) + mm_t(middle, pick) + mm_t(low, pick)

    def write(place):
        for quad in range(NB // 4):
            halves = []
            for pair in (2 * quad, 2 * quad + 1):
                first = x_ref[:, 2 * pair * BLOCK : (2 * pair + 1) * BLOCK]
                second = x_ref[:, (2 * pair + 1) * BLOCK : (2 * pair + 2) * BLOCK]
                halves.append(first + pltpu.roll(second, 2, axis=0))
            out_ref[place, quad * 16 : (quad + 1) * 16, :] = jnp.concatenate(halves, axis=0).astype(BF)

    @pl.when(backward)
    def _():
        write(SLOTS - 1)

    row_of = lax.broadcasted_iota(jnp.int32, (8, NB * BLOCK), 0)
    sign = jnp.where((row_of < 4) == jnp.logical_not(backward), 1.0, -1.0)

    def applied(values, ham):
        rounded = values.astype(BF)
        return jnp.concatenate(
            [mm(rounded, ham[:, n * 256 : (n + 1) * 256]) for n in range(NB // 2)], axis=1
        )

    def advance(step, ham):
        start = x_ref[...]
        u1 = applied(start, ham)
        u2 = applied(u1, ham) * (1.0 / 2)
        u3 = applied(u2, ham) * (1.0 / 3)
        u4 = applied(u3, ham) * (1.0 / 4)
        x_ref[...] = (start - u2 + u4) + sign * pltpu.roll(u1 - u3, 4, axis=0)
        place = jnp.where(backward, SLOTS - 2 - step, step)

        @pl.when(place >= 0)
        def _():
            write(place)

    build(0, even_h)

    def two_slots(pair, _):
        build(2 * pair + 1, odd_h)
        advance(2 * pair, even_h)
        build(2 * pair + 2, even_h)
        advance(2 * pair + 1, odd_h)
        return 0

    lax.fori_loop(0, SLOTS // 2, two_slots, 0)


def vmem():
    return pl.BlockSpec(memory_space=pltpu.VMEM)


def smem():
    return pl.BlockSpec(memory_space=pltpu.SMEM)


def chain(amps, meta, own, other, ctrl_blocks, init_states, targets):
    extent = NB * BLOCK
    return pl.pallas_call(
        chain_kernel,
        out_shape=jax.ShapeDtypeStruct((SLOTS, 64, BLOCK), BF),
        in_specs=[smem(), smem()] + [vmem()] * 5,
        out_specs=vmem(),
        scratch_shapes=[
            pltpu.VMEM((extent, extent), BF),
            pltpu.VMEM((extent, extent), BF),
            pltpu.VMEM((8, extent), jnp.float32),
            pltpu.VMEM((2 * CONTROLS, BLOCK, BLOCK), BF),
            pltpu.VMEM((2 * CONTROLS, BLOCK, BLOCK), jnp.float32),
            pltpu.VMEM((2 * CONTROLS, BLOCK, BLOCK), jnp.float32),
        ],
        compiler_params=pltpu.CompilerParams(vmem_limit_bytes=56 << 20),
        name="chain",
    )(amps, meta, own, other, ctrl_blocks, init_states, targets)


def finish_kernel(pos_ref, got_ref, ctrl_ref, states_ref, grads_ref, flat, left, right, sums):
    pick = pick_matrix(BF)
    for member in range(SLOTS):
        flat[member * 64 : (member + 1) * 64, :] = mm(got_ref[member], pick)
    for block in range(NB):
        pair, side = block // 2, block % 2
        cols = slice(block * BLOCK, (block + 1) * BLOCK)
        found = {}
        for which in range(2):
            for part in range(2):
                halves = []
                for half in range(2):
                    start = which * 512 + pair * 8 + part * 4 + side * 2 + half
                    value = flat[pl.ds(start, 8, stride=64), :]
                    if which == 0:
                        states_ref[part, half * 8 : (half + 1) * 8, cols] = value
                    halves.append(value)
                found[which, part] = jnp.concatenate(halves, axis=0)
        weights = [found[1, 0], found[1, 1]]
        source = [found[0, 1], -found[0, 0]]
        left[block] = jnp.concatenate(weights + source, axis=0).astype(BF)
        right[block] = jnp.concatenate(source + weights, axis=0)
    for k in range(CONTROLS):
        product = mm(left[pos_ref[k, 0]], ctrl_ref[k]) * right[pos_ref[k, 1]]
        sums[k : k + 1, :] = jnp.sum(product, axis=0, keepdims=True)
    ones = jnp.ones((8, BLOCK), jnp.float32)
    total = lax.dot_general(
        ones, sums[...], (((1,), (1,)), ((), ())),
        precision=lax.Precision.HIGHEST, preferred_element_type=jnp.float32,
    )
    grads_ref[...] = total[0:1, :] * (1.0 / 512)


def finish(pos, got, ctrl_blocks):
    return pl.pallas_call(
        finish_kernel,
        out_shape=(
            jax.ShapeDtypeStruct((2, 16, NB * BLOCK), jnp.float32),
            jax.ShapeDtypeStruct((1, CONTROLS), jnp.float32),
        ),
        in_specs=[smem(), vmem(), vmem()],
        out_specs=(vmem(), vmem()),
        scratch_shapes=[
            pltpu.VMEM((SLOTS * 64, BLOCK), jnp.float32),
            pltpu.VMEM((NB, 64, BLOCK), BF),
            pltpu.VMEM((NB, 64, BLOCK), jnp.float32),
            pltpu.VMEM((CONTROLS, BLOCK), jnp.float32),
        ],
        compiler_params=pltpu.CompilerParams(vmem_limit_bytes=32 << 20),
        name="finish",
    )(pos, got, ctrl_blocks)


def three_parts(values):
    high = lax.reduce_precision(values, 8, 7)
    middle = lax.reduce_precision(values - high, 8, 7)
    low = lax.reduce_precision(values - high - middle, 8, 7)
    return jnp.concatenate([high, middle, low, jnp.zeros_like(low)], axis=0).astype(BF)


def shared(values, axes, count):
    spread = jnp.broadcast_to(values[None], (count,) + values.shape)
    return lax.all_to_all(spread, axes, 0, 0)


def shards(drift, ctrl_blocks, blk_pos, amps, init_states, targets):
    member = lax.axis_index("zl") * X + lax.axis_index("x")
    twice = jnp.concatenate([drift, drift], axis=1)
    kept = lax.dynamic_slice(twice, (0, member * BLOCK), (4, KEPT * BLOCK))
    kept = jnp.einsum(
        "rjl,ml->jrm", kept.reshape(4, KEPT, BLOCK), pick_matrix(BF), preferred_element_type=BF
    )
    amps_rows = jnp.pad(three_parts(amps), ((0, 0), (0, BLOCK - CONTROLS)))
    packet = jnp.concatenate([kept, amps_rows[None]], axis=0)
    over_z = shared(packet, ("zl", "zh"), ZL * ZH)
    over_z = over_z.reshape(ZL, ZH, PIECES, 4, BLOCK).transpose(0, 2, 1, 3, 4)
    own = shared(over_z.reshape(ZL * PIECES, ZH * 4, BLOCK), ("x", "y"), X * Y)
    other = lax.ppermute(own, "c", [(0, 1), (1, 0)])
    sent = own.reshape(X, Y, ZL, PIECES, 16, BLOCK)[:, 0, :, KEPT, 0:3, 0:CONTROLS]
    amps_all = jnp.sum(sent.astype(jnp.float32), axis=2).transpose(1, 0, 2).reshape(SLOTS, CONTROLS)

    first, second = blk_pos[:, 0], blk_pos[:, 1]
    rows = jnp.concatenate([first, second])
    cols = jnp.concatenate([second, first])
    code = rows * NB + cols
    same = code[:, None] == code[None, :]
    lead = jnp.min(jnp.where(same, jnp.arange(2 * CONTROLS)[None, :], 2 * CONTROLS), axis=1)
    meta = jnp.stack([rows * BLOCK, cols * BLOCK, lead]).astype(jnp.int32)

    out = chain(amps_all, meta, own, other, ctrl_blocks, init_states, targets)
    got = lax.all_to_all(out, ("zl", "x"), 0, 0)
    states, partial_grads = finish(blk_pos, got, ctrl_blocks)
    grads = lax.psum(lax.psum(partial_grads, ("y", "c")), "zh")
    return states[None], grads


def solution(mesh):
    split = jax.sharding.Mesh(
        mesh.devices.reshape(ZL, X, Y, ZH, CORES), ("zl", "x", "y", "zh", "c")
    )
    slot, row = ("zl", "x"), ("y", "zh", "c")
    in_specs = (
        P(slot + row, None),
        P(),
        P(),
        P(slot, None),
        P(None, row, None),
        P(None, row, None),
    )
    out_specs = (P(slot, None, row, None), P(slot, None))
    return jax.shard_map(shards, mesh=split, in_specs=in_specs, out_specs=out_specs, check_vma=False)
```

```python
import functools

import jax
import jax.numpy as jnp
from jax import lax
from jax.experimental import pallas as pl
from jax.experimental.pallas import tpu as pltpu
from jax.sharding import PartitionSpec as P

ZL, X, Y, ZH, CORES = 4, 4, 4, 4, 2
BLOCK = 128
NB = 16
KEPT = NB // 2 + 1
PIECES = KEPT + 1
SLOTS = 16
CONTROLS = 16
BF = jnp.bfloat16


def source_of(index):
    r = index & 3
    zh = (index >> 2) & 3
    y = (index >> 4) & 3
    c = index >> 6
    return y * 32 + zh * 8 + c * 4 + r


def pick_matrix(dtype):
    rows = lax.broadcasted_iota(jnp.int32, (BLOCK, BLOCK), 0)
    cols = lax.broadcasted_iota(jnp.int32, (BLOCK, BLOCK), 1)
    return jnp.where(source_of(rows) == cols, 1.0, 0.0).astype(dtype)


def mm(a, b):
    return jnp.dot(a, b, preferred_element_type=jnp.float32)


def mm_t(a, b):
    return lax.dot_general(a, b, (((1,), (1,)), ((), ())), preferred_element_type=jnp.float32)


def at(start, size=BLOCK):
    return pl.ds(pl.multiple_of(start, size), size)


def this_member():
    return lax.axis_index("zl") * X + lax.axis_index("x")


def prepare_kernel(ctrl_ref, init_ref, target_ref, pieces_ref, begin_ref):
    member = this_member()
    backward = member >= SLOTS // 2
    lane = lax.rem(member, SLOTS // 2)
    pick = pick_matrix(BF)
    for k in range(CONTROLS):
        turned = mm(pick, ctrl_ref[k]).astype(BF)
        pieces_ref[k] = mm_t(turned, pick).astype(BF)
        pieces_ref[CONTROLS + k] = mm_t(pick, turned).astype(BF)

    begin_ref[...] = jnp.zeros_like(begin_ref)

    def load_from(ref):
        for part in range(2):
            for half in range(2):
                row = part * 4 + half
                begin_ref[row : row + 1, :] = ref[part, pl.ds(lane + half * 8, 1), :]

    @pl.when(backward)
    def _():
        load_from(target_ref)

    @pl.when(jnp.logical_not(backward))
    def _():
        load_from(init_ref)

    for block in range(NB):
        cols = slice(block * BLOCK, (block + 1) * BLOCK)
        value = begin_ref[:, cols]
        high = value.astype(BF)
        rest = value - high.astype(jnp.float32)
        middle = rest.astype(BF)
        low = (rest - middle.astype(jnp.float32)).astype(BF)
        begin_ref[:, cols] = mm_t(high, pick) + mm_t(middle, pick) + mm_t(low, pick)


def chain_kernel(
    amps_ref, meta_ref, own_ref, other_ref, pieces_ref, begin_ref, out_ref,
    even_h, odd_h, x_ref, base_ref, work_ref,
):
    core = lax.axis_index("c")
    backward = this_member() >= SLOTS // 2

    def lay(block_row, _):
        base = block_row * BLOCK
        zl_of = lax.div(block_row, X)
        x_of = lax.rem(block_row, X)
        for step in range(KEPT):
            col = lax.rem(block_row + step, NB) * BLOCK
            mine, theirs = (
                jnp.concatenate([ref[x_of * Y + y, zl_of * PIECES + step] for y in range(Y)], axis=0)
                for ref in (own_ref, other_ref)
            )
            first = jnp.where(core == 0, mine, theirs)
            second = jnp.where(core == 0, theirs, mine)
            block = jnp.concatenate([first, second], axis=0)
            turned = block.T if 0 < step < NB // 2 else None
            for ham in (even_h, odd_h):
                ham[at(base), at(col)] = block
                if turned is not None:
                    ham[at(col), at(base)] = turned
        return 0

    lax.fori_loop(0, NB, lay, 0)

    def gather_base(p, _):
        base_ref[p] = even_h[at(meta_ref[0, p]), at(meta_ref[1, p])]
        return 0

    lax.fori_loop(0, 2 * CONTROLS, gather_base, 0)

    def scaled(p, slot):
        lead = meta_ref[2, p]
        start = jnp.where(lead == p, base_ref[p].astype(jnp.float32), work_ref[lead])
        amp = amps_ref[slot, p % CONTROLS]
        work_ref[lead] = start + amp * pieces_ref[p].astype(jnp.float32)

    def placed(p, target):
        value = work_ref[meta_ref[2, p]].astype(BF)
        target[at(meta_ref[0, p]), at(meta_ref[1, p])] = value

    def slot_of(step):
        return jnp.where(backward, SLOTS - 1 - step, step)

    def tasks(step, target):
        slot = slot_of(jnp.minimum(step, SLOTS - 1))
        adds = [functools.partial(scaled, p, slot) for p in range(2 * CONTROLS)]
        puts = [functools.partial(placed, p, target) for p in range(2 * CONTROLS)]
        return adds + puts

    x_ref[...] = begin_ref[...]

    def write(place):
        for quad in range(NB // 4):
            halves = []
            for pair in (2 * quad, 2 * quad + 1):
                first = x_ref[:, 2 * pair * BLOCK : (2 * pair + 1) * BLOCK]
                second = x_ref[:, (2 * pair + 1) * BLOCK : (2 * pair + 2) * BLOCK]
                halves.append(first + pltpu.roll(second, 2, axis=0))
            out_ref[place, quad * 16 : (quad + 1) * 16, :] = jnp.concatenate(halves, axis=0).astype(BF)

    @pl.when(backward)
    def _():
        write(SLOTS - 1)

    row_of = lax.broadcasted_iota(jnp.int32, (8, NB * BLOCK), 0)
    sign = jnp.where((row_of < 4) == jnp.logical_not(backward), 1.0, -1.0)

    def applied(values, ham, todo):
        rounded = values.astype(BF)
        found = []
        for n in range(NB // 2):
            found.append(mm(rounded, ham[:, n * 256 : (n + 1) * 256]))
            for task in todo[2 * n : 2 * n + 2]:
                task()
        return jnp.concatenate(found, axis=1)

    def advance(step, ham, following):
        todo = tasks(step + 1, following)
        start = x_ref[...]
        u1 = applied(start, ham, todo[0:16])
        u2 = applied(u1, ham, todo[16:32]) * (1.0 / 2)
        u3 = applied(u2, ham, todo[32:48]) * (1.0 / 3)
        u4 = applied(u3, ham, todo[48:64]) * (1.0 / 4)
        x_ref[...] = (start - u2 + u4) + sign * pltpu.roll(u1 - u3, 4, axis=0)
        place = jnp.where(backward, SLOTS - 2 - step, step)

        @pl.when(place >= 0)
        def _():
            write(place)

    for task in tasks(0, even_h):
        task()

    def two_slots(pair, _):
        advance(2 * pair, even_h, odd_h)
        advance(2 * pair + 1, odd_h, even_h)
        return 0

    lax.fori_loop(0, SLOTS // 2, two_slots, 0)


def vmem():
    return pl.BlockSpec(memory_space=pltpu.VMEM)


def smem():
    return pl.BlockSpec(memory_space=pltpu.SMEM)


def prepare(ctrl_blocks, init_states, targets):
    return pl.pallas_call(
        prepare_kernel,
        out_shape=(
            jax.ShapeDtypeStruct((2 * CONTROLS, BLOCK, BLOCK), BF),
            jax.ShapeDtypeStruct((8, NB * BLOCK), jnp.float32),
        ),
        in_specs=[vmem()] * 3,
        out_specs=(vmem(), vmem()),
        compiler_params=pltpu.CompilerParams(vmem_limit_bytes=16 << 20),
        cost_estimate=pl.CostEstimate(
            flops=2 * 3 * CONTROLS * BLOCK**3, bytes_accessed=8 << 20, transcendentals=0
        ),
        name="prepare",
    )(ctrl_blocks, init_states, targets)


def chain(amps, meta, own, other, pieces, begin):
    extent = NB * BLOCK
    return pl.pallas_call(
        chain_kernel,
        out_shape=jax.ShapeDtypeStruct((SLOTS, 64, BLOCK), BF),
        in_specs=[smem(), smem()] + [vmem()] * 4,
        out_specs=vmem(),
        scratch_shapes=[
            pltpu.VMEM((extent, extent), BF),
            pltpu.VMEM((extent, extent), BF),
            pltpu.VMEM((8, extent), jnp.float32),
            pltpu.VMEM((2 * CONTROLS, BLOCK, BLOCK), BF),
            pltpu.VMEM((2 * CONTROLS, BLOCK, BLOCK), jnp.float32),
        ],
        compiler_params=pltpu.CompilerParams(vmem_limit_bytes=30 << 20),
        cost_estimate=pl.CostEstimate(
            flops=2 * 8 * 64 * extent**2, bytes_accessed=8 << 20, transcendentals=0
        ),
        name="chain",
    )(amps, meta, own, other, pieces, begin)


def finish_kernel(pos_ref, got_ref, ctrl_ref, states_ref, grads_ref, flat, left, right, sums):
    pick = pick_matrix(BF)
    for member in range(SLOTS):
        flat[member * 64 : (member + 1) * 64, :] = mm(got_ref[member], pick)
    for block in range(NB):
        pair, side = block // 2, block % 2
        cols = slice(block * BLOCK, (block + 1) * BLOCK)
        found = {}
        for which in range(2):
            for part in range(2):
                halves = []
                for half in range(2):
                    start = which * 512 + pair * 8 + part * 4 + side * 2 + half
                    value = flat[pl.ds(start, 8, stride=64), :]
                    if which == 0:
                        states_ref[part, half * 8 : (half + 1) * 8, cols] = value
                    halves.append(value)
                found[which, part] = jnp.concatenate(halves, axis=0)
        weights = [found[1, 0], found[1, 1]]
        source = [found[0, 1], -found[0, 0]]
        left[block] = jnp.concatenate(weights + source, axis=0).astype(BF)
        right[block] = jnp.concatenate(source + weights, axis=0)
    for k in range(CONTROLS):
        product = mm(left[pos_ref[k, 0]], ctrl_ref[k]) * right[pos_ref[k, 1]]
        sums[k : k + 1, :] = jnp.sum(product, axis=0, keepdims=True)
    ones = jnp.ones((8, BLOCK), jnp.float32)
    total = lax.dot_general(
        ones, sums[...], (((1,), (1,)), ((), ())),
        precision=lax.Precision.HIGHEST, preferred_element_type=jnp.float32,
    )
    grads_ref[...] = total[0:1, :] * (1.0 / 512)


def finish(pos, got, ctrl_blocks):
    return pl.pallas_call(
        finish_kernel,
        out_shape=(
            jax.ShapeDtypeStruct((2, 16, NB * BLOCK), jnp.float32),
            jax.ShapeDtypeStruct((1, CONTROLS), jnp.float32),
        ),
        in_specs=[smem(), vmem(), vmem()],
        out_specs=(vmem(), vmem()),
        scratch_shapes=[
            pltpu.VMEM((SLOTS * 64, BLOCK), jnp.float32),
            pltpu.VMEM((NB, 64, BLOCK), BF),
            pltpu.VMEM((NB, 64, BLOCK), jnp.float32),
            pltpu.VMEM((CONTROLS, BLOCK), jnp.float32),
        ],
        compiler_params=pltpu.CompilerParams(vmem_limit_bytes=32 << 20),
        name="finish",
    )(pos, got, ctrl_blocks)


def three_parts(values):
    high = lax.reduce_precision(values, 8, 7)
    middle = lax.reduce_precision(values - high, 8, 7)
    low = lax.reduce_precision(values - high - middle, 8, 7)
    return jnp.concatenate([high, middle, low, jnp.zeros_like(low)], axis=0).astype(BF)


def shared(values, axes, count):
    spread = jnp.broadcast_to(values[None], (count,) + values.shape)
    return lax.all_to_all(spread, axes, 0, 0)


def shards(drift, ctrl_blocks, blk_pos, amps, init_states, targets):
    member = this_member()
    pieces, begin = prepare(ctrl_blocks, init_states, targets)
    twice = jnp.concatenate([drift, drift], axis=1)
    kept = lax.dynamic_slice(twice, (0, member * BLOCK), (4, KEPT * BLOCK))
    kept = jnp.einsum(
        "rjl,ml->jrm", kept.reshape(4, KEPT, BLOCK), pick_matrix(BF), preferred_element_type=BF
    )
    amps_rows = jnp.pad(three_parts(amps), ((0, 0), (0, BLOCK - CONTROLS)))
    packet = jnp.concatenate([kept, amps_rows[None]], axis=0)
    over_z = shared(packet, ("zl", "zh"), ZL * ZH)
    over_z = over_z.reshape(ZL, ZH, PIECES, 4, BLOCK).transpose(0, 2, 1, 3, 4)
    own = shared(over_z.reshape(ZL * PIECES, ZH * 4, BLOCK), ("x", "y"), X * Y)
    other = lax.ppermute(own, "c", [(0, 1), (1, 0)])
    sent = own.reshape(X, Y, ZL, PIECES, 16, BLOCK)[:, 0, :, KEPT, 0:3, 0:CONTROLS]
    amps_all = jnp.sum(sent.astype(jnp.float32), axis=2).transpose(1, 0, 2).reshape(SLOTS, CONTROLS)

    first, second = blk_pos[:, 0], blk_pos[:, 1]
    rows = jnp.concatenate([first, second])
    cols = jnp.concatenate([second, first])
    code = rows * NB + cols
    same = code[:, None] == code[None, :]
    lead = jnp.min(jnp.where(same, jnp.arange(2 * CONTROLS)[None, :], 2 * CONTROLS), axis=1)
    meta = jnp.stack([rows * BLOCK, cols * BLOCK, lead]).astype(jnp.int32)

    out = chain(amps_all, meta, own, other, pieces, begin)
    got = lax.all_to_all(out, ("zl", "x"), 0, 0)
    states, partial_grads = finish(blk_pos, got, ctrl_blocks)
    grads = lax.psum(lax.psum(partial_grads, ("y", "c")), "zh")
    return states[None], grads


def solution(mesh):
    split = jax.sharding.Mesh(
        mesh.devices.reshape(ZL, X, Y, ZH, CORES), ("zl", "x", "y", "zh", "c")
    )
    slot, row = ("zl", "x"), ("y", "zh", "c")
    in_specs = (
        P(slot + row, None),
        P(),
        P(),
        P(slot, None),
        P(None, row, None),
        P(None, row, None),
    )
    out_specs = (P(slot, None, row, None), P(slot, None))
    return jax.shard_map(shards, mesh=split, in_specs=in_specs, out_specs=out_specs, check_vma=False)
```

```python
import functools

import jax
import jax.numpy as jnp
from jax import lax
from jax.experimental import pallas as pl
from jax.experimental.pallas import tpu as pltpu
from jax.sharding import PartitionSpec as P

ZL, X, Y, ZH, CORES = 4, 4, 4, 4, 2
BLOCK = 128
NB = 16
KEPT = NB // 2 + 1
HALF = BLOCK // 2
SLOTS = 16
CONTROLS = 16
BF = jnp.bfloat16


def source_of(index):
    r = index & 3
    zh = (index >> 2) & 3
    y = (index >> 4) & 3
    c = index >> 6
    return y * 32 + zh * 8 + c * 4 + r


def pick_matrix(dtype):
    rows = lax.broadcasted_iota(jnp.int32, (BLOCK, BLOCK), 0)
    cols = lax.broadcasted_iota(jnp.int32, (BLOCK, BLOCK), 1)
    return jnp.where(source_of(rows) == cols, 1.0, 0.0).astype(dtype)


def mm(a, b):
    return jnp.dot(a, b, preferred_element_type=jnp.float32)


def mm_t(a, b):
    return lax.dot_general(a, b, (((1,), (1,)), ((), ())), preferred_element_type=jnp.float32)


def at(start, size=BLOCK):
    return pl.ds(pl.multiple_of(start, size), size)


def this_member():
    return lax.axis_index("zl") * X + lax.axis_index("x")


def kept_half(member, core):
    return jnp.where(member < SLOTS // 2, core, 1 - core)


def source_kernel(drift_ref, amps_ref, packet_ref):
    member = this_member()
    pick = pick_matrix(BF)
    for step in range(KEPT - 1):
        block = lax.rem(member + step, NB)
        packet_ref[step] = mm_t(drift_ref[:, at(block * BLOCK)], pick).astype(BF)
    block = lax.rem(member + KEPT - 1, NB)
    kept = mm_t(drift_ref[:, at(block * BLOCK)], pick)
    row = lax.broadcasted_iota(jnp.int32, (4, BLOCK), 0)
    lane = lax.broadcasted_iota(jnp.int32, (4, BLOCK), 1)
    amps = amps_ref[...]
    high = amps.astype(BF).astype(jnp.float32)
    middle = (amps - high).astype(BF).astype(jnp.float32)
    low = amps - high - middle
    parts = jnp.where(row == 0, high, jnp.where(row == 1, middle, jnp.where(row == 2, low, 0.0)))
    mine = (lane >= HALF) == (kept_half(member, lax.axis_index("c")) == 1)
    packet_ref[KEPT - 1] = jnp.where(mine, kept, parts).astype(BF)


def prepare_kernel(ctrl_ref, init_ref, target_ref, pieces_ref, begin_ref):
    member = this_member()
    backward = member >= SLOTS // 2
    lane = lax.rem(member, SLOTS // 2)
    pick = pick_matrix(BF)
    for k in range(CONTROLS):
        turned = mm(pick, ctrl_ref[k]).astype(BF)
        pieces_ref[k] = mm_t(turned, pick).astype(BF)
        pieces_ref[CONTROLS + k] = mm_t(pick, turned).astype(BF)

    begin_ref[...] = jnp.zeros_like(begin_ref)

    def load_from(ref):
        for part in range(2):
            for half in range(2):
                row = part * 4 + half
                begin_ref[row : row + 1, :] = ref[part, pl.ds(lane + half * 8, 1), :]

    @pl.when(backward)
    def _():
        load_from(target_ref)

    @pl.when(jnp.logical_not(backward))
    def _():
        load_from(init_ref)

    for block in range(NB):
        cols = slice(block * BLOCK, (block + 1) * BLOCK)
        value = begin_ref[:, cols]
        high = value.astype(BF)
        rest = value - high.astype(jnp.float32)
        middle = rest.astype(BF)
        low = (rest - middle.astype(jnp.float32)).astype(BF)
        begin_ref[:, cols] = mm_t(high, pick) + mm_t(middle, pick) + mm_t(low, pick)


def chain_kernel(
    amps_ref, meta_ref, own_ref, other_ref, pieces_ref, begin_ref, out_ref,
    even_h, odd_h, x_ref, base_ref,
):
    core = lax.axis_index("c")
    backward = this_member() >= SLOTS // 2

    def piece(block_row, step):
        zl_of = lax.div(block_row, X)
        x_of = lax.rem(block_row, X)
        mine, theirs = (
            jnp.concatenate([ref[x_of * Y + y, zl_of * KEPT + step] for y in range(Y)], axis=0)
            for ref in (own_ref, other_ref)
        )
        first = jnp.where(core == 0, mine, theirs)
        second = jnp.where(core == 0, theirs, mine)
        return jnp.concatenate([first, second], axis=0)

    def put(row, col, block):
        for ham in (even_h, odd_h):
            ham[at(row * BLOCK), at(col * BLOCK)] = block

    def lay(block_row, _):
        put(block_row, block_row, piece(block_row, 0))
        for step in range(1, KEPT - 1):
            col = lax.rem(block_row + step, NB)
            block = piece(block_row, step)
            put(block_row, col, block)
            put(col, block_row, block.T)
        return 0

    lax.fori_loop(0, NB, lay, 0)
    low_row = lax.broadcasted_iota(jnp.int32, (BLOCK, BLOCK), 0) < HALF
    low_col = lax.broadcasted_iota(jnp.int32, (BLOCK, BLOCK), 1) < HALF
    diagonal = jnp.where(low_row == low_col, 1.0, 0.0).astype(BF)
    crossed = jnp.where(low_row == low_col, 0.0, 1.0).astype(BF)

    def lay_shared(block_row, _):
        col = block_row + NB // 2
        upper, lower = piece(block_row, KEPT - 1), piece(col, KEPT - 1)
        put(block_row, col, upper * diagonal + lower.T * crossed)
        put(col, block_row, upper.T * diagonal + lower * crossed)
        return 0

    lax.fori_loop(0, NB // 2, lay_shared, 0, unroll=2)

    def gather_base(p, _):
        base_ref[p] = even_h[at(meta_ref[0, p]), at(meta_ref[1, p])]
        return 0

    lax.fori_loop(0, 2 * CONTROLS, gather_base, 0)

    def slot_of(step):
        return jnp.where(backward, SLOTS - 1 - step, step)

    def tasks(step, target):
        slot = slot_of(jnp.minimum(step, SLOTS - 1))
        total = [None]

        def task(p):
            which = meta_ref[2, p]
            start = base_ref[p].astype(jnp.float32)
            if p > 0:
                start = jnp.where(meta_ref[3, p] == 0, start, total[0])
            amp = amps_ref[slot, lax.rem(which, CONTROLS)]
            total[0] = start + amp * pieces_ref[which].astype(jnp.float32)
            target[at(meta_ref[0, p]), at(meta_ref[1, p])] = total[0].astype(BF)

        return [functools.partial(task, p) for p in range(2 * CONTROLS)]

    x_ref[...] = begin_ref[...]

    def write(place):
        for quad in range(NB // 4):
            halves = []
            for pair in (2 * quad, 2 * quad + 1):
                first = x_ref[:, 2 * pair * BLOCK : (2 * pair + 1) * BLOCK]
                second = x_ref[:, (2 * pair + 1) * BLOCK : (2 * pair + 2) * BLOCK]
                halves.append(first + pltpu.roll(second, 2, axis=0))
            out_ref[place, quad * 16 : (quad + 1) * 16, :] = jnp.concatenate(halves, axis=0).astype(BF)

    @pl.when(backward)
    def _():
        write(SLOTS - 1)

    row_of = lax.broadcasted_iota(jnp.int32, (8, NB * BLOCK), 0)
    sign = jnp.where((row_of < 4) == jnp.logical_not(backward), 1.0, -1.0)

    def applied(values, ham, todo):
        rounded = values.astype(BF)
        found = []
        for n in range(NB // 2):
            found.append(mm(rounded, ham[:, n * 256 : (n + 1) * 256]))
            for task in todo[n : n + 1]:
                task()
        return jnp.concatenate(found, axis=1)

    def advance(step, ham, following):
        todo = tasks(step + 1, following)
        start = x_ref[...]
        u1 = applied(start, ham, todo[0:8])
        u2 = applied(u1, ham, todo[8:16]) * (1.0 / 2)
        u3 = applied(u2, ham, todo[16:24]) * (1.0 / 3)
        u4 = applied(u3, ham, todo[24:32]) * (1.0 / 4)
        x_ref[...] = (start - u2 + u4) + sign * pltpu.roll(u1 - u3, 4, axis=0)
        place = jnp.where(backward, SLOTS - 2 - step, step)

        @pl.when(place >= 0)
        def _():
            write(place)

    for task in tasks(0, even_h):
        task()

    def two_slots(pair, _):
        advance(2 * pair, even_h, odd_h)
        advance(2 * pair + 1, odd_h, even_h)
        return 0

    lax.fori_loop(0, SLOTS // 2, two_slots, 0)


def vmem():
    return pl.BlockSpec(memory_space=pltpu.VMEM)


def smem():
    return pl.BlockSpec(memory_space=pltpu.SMEM)


def source(drift, amps):
    return pl.pallas_call(
        source_kernel,
        out_shape=jax.ShapeDtypeStruct((KEPT, 4, BLOCK), BF),
        in_specs=[vmem(), vmem()],
        out_specs=vmem(),
        compiler_params=pltpu.CompilerParams(vmem_limit_bytes=2 << 20),
        name="source",
    )(drift, jnp.pad(jnp.concatenate([amps] * 2), ((0, 0), (0, HALF - CONTROLS))).reshape(1, BLOCK))


def prepare(ctrl_blocks, init_states, targets):
    return pl.pallas_call(
        prepare_kernel,
        out_shape=(
            jax.ShapeDtypeStruct((2 * CONTROLS, BLOCK, BLOCK), BF),
            jax.ShapeDtypeStruct((8, NB * BLOCK), jnp.float32),
        ),
        in_specs=[vmem()] * 3,
        out_specs=(vmem(), vmem()),
        compiler_params=pltpu.CompilerParams(vmem_limit_bytes=6 << 20),
        cost_estimate=pl.CostEstimate(
            flops=2 * 3 * CONTROLS * BLOCK**3, bytes_accessed=8 << 20, transcendentals=0
        ),
        name="prepare",
    )(ctrl_blocks, init_states, targets)


def chain(amps, meta, own, other, pieces, begin):
    extent = NB * BLOCK
    return pl.pallas_call(
        chain_kernel,
        out_shape=jax.ShapeDtypeStruct((SLOTS, 64, BLOCK), BF),
        in_specs=[smem(), smem()] + [vmem()] * 4,
        out_specs=vmem(),
        scratch_shapes=[
            pltpu.VMEM((extent, extent), BF),
            pltpu.VMEM((extent, extent), BF),
            pltpu.VMEM((8, extent), jnp.float32),
            pltpu.VMEM((2 * CONTROLS, BLOCK, BLOCK), BF),
        ],
        compiler_params=pltpu.CompilerParams(vmem_limit_bytes=30 << 20),
        cost_estimate=pl.CostEstimate(
            flops=2 * 8 * 64 * extent**2, bytes_accessed=8 << 20, transcendentals=0
        ),
        name="chain",
    )(amps, meta, own, other, pieces, begin)


def finish_kernel(pos_ref, got_ref, ctrl_ref, states_ref, grads_ref, flat, left, right, sums):
    pick = pick_matrix(BF)
    for member in range(SLOTS):
        flat[member * 64 : (member + 1) * 64, :] = mm(got_ref[member], pick)
    for block in range(NB):
        pair, side = block // 2, block % 2
        cols = slice(block * BLOCK, (block + 1) * BLOCK)
        found = {}
        for which in range(2):
            for part in range(2):
                halves = []
                for half in range(2):
                    start = which * 512 + pair * 8 + part * 4 + side * 2 + half
                    value = flat[pl.ds(start, 8, stride=64), :]
                    if which == 0:
                        states_ref[part, half * 8 : (half + 1) * 8, cols] = value
                    halves.append(value)
                found[which, part] = jnp.concatenate(halves, axis=0)
        weights = [found[1, 0], found[1, 1]]
        source = [found[0, 1], -found[0, 0]]
        left[block] = jnp.concatenate(weights + source, axis=0).astype(BF)
        right[block] = jnp.concatenate(source + weights, axis=0)
    for k in range(CONTROLS):
        product = mm(left[pos_ref[k, 0]], ctrl_ref[k]) * right[pos_ref[k, 1]]
        sums[k : k + 1, :] = jnp.sum(product, axis=0, keepdims=True)
    ones = jnp.ones((8, BLOCK), jnp.float32)
    total = lax.dot_general(
        ones, sums[...], (((1,), (1,)), ((), ())),
        precision=lax.Precision.HIGHEST, preferred_element_type=jnp.float32,
    )
    grads_ref[...] = total[0:1, :] * (1.0 / 512)


def finish(pos, got, ctrl_blocks):
    return pl.pallas_call(
        finish_kernel,
        out_shape=(
            jax.ShapeDtypeStruct((2, 16, NB * BLOCK), jnp.float32),
            jax.ShapeDtypeStruct((1, CONTROLS), jnp.float32),
        ),
        in_specs=[smem(), vmem(), vmem()],
        out_specs=(vmem(), vmem()),
        scratch_shapes=[
            pltpu.VMEM((SLOTS * 64, BLOCK), jnp.float32),
            pltpu.VMEM((NB, 64, BLOCK), BF),
            pltpu.VMEM((NB, 64, BLOCK), jnp.float32),
            pltpu.VMEM((CONTROLS, BLOCK), jnp.float32),
        ],
        compiler_params=pltpu.CompilerParams(vmem_limit_bytes=8 << 20),
        name="finish",
    )(pos, got, ctrl_blocks)


def shared(values, axes, count):
    spread = jnp.broadcast_to(values[None], (count,) + values.shape)
    return lax.all_to_all(spread, axes, 0, 0)


def shards(drift, ctrl_blocks, blk_pos, amps, init_states, targets):
    pieces, begin = prepare(ctrl_blocks, init_states, targets)
    over_z = shared(source(drift, amps), ("zl", "zh"), ZL * ZH)
    over_z = over_z.reshape(ZL, ZH, KEPT, 4, BLOCK).transpose(0, 2, 1, 3, 4)
    own = shared(over_z.reshape(ZL * KEPT, ZH * 4, BLOCK), ("x", "y"), X * Y)
    other = lax.ppermute(own, "c", [(0, 1), (1, 0)])
    sent = own.reshape(X, Y, ZL, KEPT, 16, BLOCK)[:, 0, :, KEPT - 1, 0:3]
    sent = jnp.sum(sent.astype(jnp.float32), axis=2).transpose(1, 0, 2).reshape(SLOTS, BLOCK)
    free = 1 - kept_half(jnp.arange(SLOTS)[:, None], lax.axis_index("c"))
    amps_all = jnp.where(free == 0, sent[:, 0:CONTROLS], sent[:, HALF : HALF + CONTROLS])

    rows = jnp.concatenate([blk_pos[:, 0], blk_pos[:, 1]])
    cols = jnp.concatenate([blk_pos[:, 1], blk_pos[:, 0]])
    number = jnp.arange(2 * CONTROLS)
    key = (rows * NB + cols) * (2 * CONTROLS) + number
    rank = jnp.sum(key[None, :] < key[:, None], axis=1)
    chosen = rank[None, :] == number[:, None]
    key = jnp.sum(jnp.where(chosen, key[None, :], 0), axis=1)
    place = key // (2 * CONTROLS)
    again = jnp.concatenate([jnp.zeros((1,), bool), place[1:] == place[:-1]])
    meta = jnp.stack([place // NB * BLOCK, place % NB * BLOCK, key % (2 * CONTROLS), again])
    meta = meta.astype(jnp.int32)

    out = chain(amps_all, meta, own, other, pieces, begin)
    got = lax.all_to_all(out, ("zl", "x"), 0, 0)
    states, partial_grads = finish(blk_pos, got, ctrl_blocks)
    grads = jnp.sum(shared(partial_grads, ("y", "zh", "c"), Y * ZH * CORES), axis=0)
    return states[None], grads


def solution(mesh):
    split = jax.sharding.Mesh(
        mesh.devices.reshape(ZL, X, Y, ZH, CORES), ("zl", "x", "y", "zh", "c")
    )
    slot, row = ("zl", "x"), ("y", "zh", "c")
    in_specs = (
        P(slot + row, None),
        P(),
        P(),
        P(slot, None),
        P(None, row, None),
        P(None, row, None),
    )
    out_specs = (P(slot, None, row, None), P(slot, None))
    return jax.shard_map(shards, mesh=split, in_specs=in_specs, out_specs=out_specs, check_vma=False)
```

```python
import functools

import jax
import jax.numpy as jnp
from jax import lax
from jax.experimental import pallas as pl
from jax.experimental.pallas import tpu as pltpu
from jax.sharding import PartitionSpec as P

ZL, X, Y, ZH, CORES = 4, 4, 4, 4, 2
BLOCK = 128
NB = 16
KEPT = NB // 2 + 1
HALF = BLOCK // 2
SLOTS = 16
CONTROLS = 16
BF = jnp.bfloat16


def source_of(index):
    r = index & 3
    zh = (index >> 2) & 3
    y = (index >> 4) & 3
    c = index >> 6
    return y * 32 + zh * 8 + c * 4 + r


def pick_matrix(dtype):
    rows = lax.broadcasted_iota(jnp.int32, (BLOCK, BLOCK), 0)
    cols = lax.broadcasted_iota(jnp.int32, (BLOCK, BLOCK), 1)
    return jnp.where(source_of(rows) == cols, 1.0, 0.0).astype(dtype)


def mm(a, b):
    return jnp.dot(a, b, preferred_element_type=jnp.float32)


def mm_t(a, b):
    return lax.dot_general(a, b, (((1,), (1,)), ((), ())), preferred_element_type=jnp.float32)


def at(start, size=BLOCK):
    return pl.ds(pl.multiple_of(start, size), size)


def this_member():
    return lax.axis_index("zl") * X + lax.axis_index("x")


def kept_half(member, core):
    return jnp.where(member < SLOTS // 2, core, 1 - core)


def source_kernel(drift_ref, amps_ref, packet_ref):
    member = this_member()
    pick = pick_matrix(BF)
    for step in range(KEPT - 1):
        block = lax.rem(member + step, NB)
        packet_ref[step] = mm_t(drift_ref[:, at(block * BLOCK)], pick).astype(BF)
    block = lax.rem(member + KEPT - 1, NB)
    kept = mm_t(drift_ref[:, at(block * BLOCK)], pick)
    lane = lax.broadcasted_iota(jnp.int32, (4, BLOCK), 1)
    amps = amps_ref[...]
    high = amps.astype(BF).astype(jnp.float32)
    middle = (amps - high).astype(BF).astype(jnp.float32)
    low = amps - high - middle
    part = lax.broadcasted_iota(jnp.int32, (4, CONTROLS), 0)
    parts = jnp.where(part == 0, high, jnp.where(part == 1, middle, jnp.where(part == 2, low, 0.0)))
    number = lax.broadcasted_iota(jnp.int32, (CONTROLS, BLOCK), 0)
    column = lax.broadcasted_iota(jnp.int32, (CONTROLS, BLOCK), 1)
    spread = jnp.where((column & (HALF - 1)) == number, 1.0, 0.0).astype(BF)
    parts = mm(parts.astype(BF), spread)
    mine = (lane >= HALF) == (kept_half(member, lax.axis_index("c")) == 1)
    packet_ref[KEPT - 1] = jnp.where(mine, kept, parts).astype(BF)


def prepare_kernel(ctrl_ref, init_ref, target_ref, pieces_ref, begin_ref):
    member = this_member()
    backward = member >= SLOTS // 2
    lane = lax.rem(member, SLOTS // 2)
    pick = pick_matrix(BF)
    for k in range(CONTROLS):
        turned = mm(pick, ctrl_ref[k]).astype(BF)
        pieces_ref[k] = mm_t(turned, pick).astype(BF)
        pieces_ref[CONTROLS + k] = mm_t(pick, turned).astype(BF)

    begin_ref[...] = jnp.zeros_like(begin_ref)

    def load_from(ref):
        for part in range(2):
            for half in range(2):
                row = part * 4 + half
                begin_ref[row : row + 1, :] = ref[part, pl.ds(lane + half * 8, 1), :]

    @pl.when(backward)
    def _():
        load_from(target_ref)

    @pl.when(jnp.logical_not(backward))
    def _():
        load_from(init_ref)

    for block in range(NB):
        cols = slice(block * BLOCK, (block + 1) * BLOCK)
        value = begin_ref[:, cols]
        high = value.astype(BF)
        rest = value - high.astype(jnp.float32)
        middle = rest.astype(BF)
        low = (rest - middle.astype(jnp.float32)).astype(BF)
        begin_ref[:, cols] = mm_t(high, pick) + mm_t(middle, pick) + mm_t(low, pick)


def chain_kernel(
    amps_ref, meta_ref, own_ref, sent_ref, pieces_ref, begin_ref, out_ref,
    even_h, odd_h, x_ref, base_ref, other_ref, sems,
):
    core = lax.axis_index("c")
    backward = this_member() >= SLOTS // 2

    def piece(block_row, step):
        zl_of = lax.div(block_row, X)
        x_of = lax.rem(block_row, X)
        mine, theirs = (
            jnp.concatenate([ref[x_of * Y + y, zl_of * KEPT + step] for y in range(Y)], axis=0)
            for ref in (own_ref, other_ref)
        )
        first = jnp.where(core == 0, mine, theirs)
        second = jnp.where(core == 0, theirs, mine)
        return jnp.concatenate([first, second], axis=0)

    def put(row, col, block):
        for ham in (even_h, odd_h):
            ham[at(row * BLOCK), at(col * BLOCK)] = block

    def lay(block_row):
        put(block_row, block_row, piece(block_row, 0))
        for step in range(1, KEPT - 1):
            col = lax.rem(block_row + step, NB)
            block = piece(block_row, step)
            put(block_row, col, block)
            put(col, block_row, block.T)

    def fetch(x_of):
        part = pl.ds(x_of * Y, Y)
        return pltpu.make_async_copy(sent_ref.at[part], other_ref.at[part], sems.at[x_of])

    for x_of in range(X):
        fetch(x_of).start()
    for x_of in range(X):
        fetch(x_of).wait()

        def lay_next(zl_of, _, x_of=x_of):
            lay(zl_of * X + x_of)
            return 0

        lax.fori_loop(0, ZL, lay_next, 0)

    low_row = lax.broadcasted_iota(jnp.int32, (BLOCK, BLOCK), 0) < HALF
    low_col = lax.broadcasted_iota(jnp.int32, (BLOCK, BLOCK), 1) < HALF
    diagonal = jnp.where(low_row == low_col, 1.0, 0.0).astype(BF)
    crossed = jnp.where(low_row == low_col, 0.0, 1.0).astype(BF)

    def lay_shared(block_row, _):
        col = block_row + NB // 2
        upper, lower = piece(block_row, KEPT - 1), piece(col, KEPT - 1)
        put(block_row, col, upper * diagonal + lower.T * crossed)
        put(col, block_row, upper.T * diagonal + lower * crossed)
        return 0

    lax.fori_loop(0, NB // 2, lay_shared, 0, unroll=2)

    def gather_base(p, _):
        base_ref[p] = even_h[at(meta_ref[0, p]), at(meta_ref[1, p])]
        return 0

    lax.fori_loop(0, 2 * CONTROLS, gather_base, 0)

    def slot_of(step):
        return jnp.where(backward, SLOTS - 1 - step, step)

    def tasks(step, target):
        slot = slot_of(jnp.minimum(step, SLOTS - 1))
        total = [None]

        def task(p):
            which = meta_ref[2, p]
            start = base_ref[p].astype(jnp.float32)
            if p > 0:
                start = jnp.where(meta_ref[3, p] == 0, start, total[0])
            amp = amps_ref[slot, lax.rem(which, CONTROLS)]
            total[0] = start + amp * pieces_ref[which].astype(jnp.float32)
            target[at(meta_ref[0, p]), at(meta_ref[1, p])] = total[0].astype(BF)

        return [functools.partial(task, p) for p in range(2 * CONTROLS)]

    x_ref[...] = begin_ref[...]

    def write(place):
        for quad in range(NB // 4):
            halves = []
            for pair in (2 * quad, 2 * quad + 1):
                first = x_ref[:, 2 * pair * BLOCK : (2 * pair + 1) * BLOCK]
                second = x_ref[:, (2 * pair + 1) * BLOCK : (2 * pair + 2) * BLOCK]
                halves.append(first + pltpu.roll(second, 2, axis=0))
            out_ref[place, quad * 16 : (quad + 1) * 16, :] = jnp.concatenate(halves, axis=0).astype(BF)

    @pl.when(backward)
    def _():
        write(SLOTS - 1)

    row_of = lax.broadcasted_iota(jnp.int32, (8, NB * BLOCK), 0)
    sign = jnp.where((row_of < 4) == jnp.logical_not(backward), 1.0, -1.0)

    def applied(values, ham, todo):
        rounded = values.astype(BF)
        found = []
        for n in range(NB // 2):
            found.append(mm(rounded, ham[:, n * 256 : (n + 1) * 256]))
            for task in todo[n : n + 1]:
                task()
        return jnp.concatenate(found, axis=1)

    def advance(step, ham, following):
        todo = tasks(step + 1, following)
        start = x_ref[...]
        u1 = applied(start, ham, todo[0:8])
        u2 = applied(u1, ham, todo[8:16]) * (1.0 / 2)
        u3 = applied(u2, ham, todo[16:24]) * (1.0 / 3)
        u4 = applied(u3, ham, todo[24:32]) * (1.0 / 4)
        x_ref[...] = (start - u2 + u4) + sign * pltpu.roll(u1 - u3, 4, axis=0)
        place = jnp.where(backward, SLOTS - 2 - step, step)

        @pl.when(place >= 0)
        def _():
            write(place)

    for task in tasks(0, even_h):
        task()

    def two_slots(pair, _):
        advance(2 * pair, even_h, odd_h)
        advance(2 * pair + 1, odd_h, even_h)
        return 0

    lax.fori_loop(0, SLOTS // 2, two_slots, 0)


def vmem():
    return pl.BlockSpec(memory_space=pltpu.VMEM)


def smem():
    return pl.BlockSpec(memory_space=pltpu.SMEM)


def source(drift, amps):
    return pl.pallas_call(
        source_kernel,
        out_shape=jax.ShapeDtypeStruct((KEPT, 4, BLOCK), BF),
        in_specs=[vmem(), vmem()],
        out_specs=vmem(),
        compiler_params=pltpu.CompilerParams(vmem_limit_bytes=2 << 20),
        name="source",
    )(drift, amps)


def prepare(ctrl_blocks, init_states, targets):
    return pl.pallas_call(
        prepare_kernel,
        out_shape=(
            jax.ShapeDtypeStruct((2 * CONTROLS, BLOCK, BLOCK), BF),
            jax.ShapeDtypeStruct((8, NB * BLOCK), jnp.float32),
        ),
        in_specs=[vmem()] * 3,
        out_specs=(vmem(), vmem()),
        compiler_params=pltpu.CompilerParams(vmem_limit_bytes=6 << 20),
        cost_estimate=pl.CostEstimate(
            flops=2 * 3 * CONTROLS * BLOCK**3, bytes_accessed=8 << 20, transcendentals=0
        ),
        name="prepare",
    )(ctrl_blocks, init_states, targets)


def chain(amps, meta, own, other, pieces, begin):
    extent = NB * BLOCK
    return pl.pallas_call(
        chain_kernel,
        out_shape=jax.ShapeDtypeStruct((SLOTS, 64, BLOCK), BF),
        in_specs=[smem(), smem(), vmem(), pl.BlockSpec(memory_space=pl.ANY), vmem(), vmem()],
        out_specs=vmem(),
        scratch_shapes=[
            pltpu.VMEM((extent, extent), BF),
            pltpu.VMEM((extent, extent), BF),
            pltpu.VMEM((8, extent), jnp.float32),
            pltpu.VMEM((2 * CONTROLS, BLOCK, BLOCK), BF),
            pltpu.VMEM((X * Y, ZL * KEPT, 16, BLOCK), BF),
            pltpu.SemaphoreType.DMA((X,)),
        ],
        compiler_params=pltpu.CompilerParams(vmem_limit_bytes=30 << 20),
        cost_estimate=pl.CostEstimate(
            flops=2 * 8 * 64 * extent**2, bytes_accessed=8 << 20, transcendentals=0
        ),
        name="chain",
    )(amps, meta, own, other, pieces, begin)


def finish_kernel(pos_ref, got_ref, ctrl_ref, states_ref, grads_ref, flat, left, right, sums):
    pick = pick_matrix(BF)
    for member in range(SLOTS):
        flat[member * 64 : (member + 1) * 64, :] = mm(got_ref[member], pick)
    for block in range(NB):
        pair, side = block // 2, block % 2
        cols = slice(block * BLOCK, (block + 1) * BLOCK)
        found = {}
        for which in range(2):
            for part in range(2):
                halves = []
                for half in range(2):
                    start = which * 512 + pair * 8 + part * 4 + side * 2 + half
                    value = flat[pl.ds(start, 8, stride=64), :]
                    if which == 0:
                        states_ref[part, half * 8 : (half + 1) * 8, cols] = value
                    halves.append(value)
                found[which, part] = jnp.concatenate(halves, axis=0)
        weights = [found[1, 0], found[1, 1]]
        source = [found[0, 1], -found[0, 0]]
        left[block] = jnp.concatenate(weights + source, axis=0).astype(BF)
        right[block] = jnp.concatenate(source + weights, axis=0)
    for k in range(CONTROLS):
        product = mm(left[pos_ref[k, 0]], ctrl_ref[k]) * right[pos_ref[k, 1]]
        sums[k : k + 1, :] = jnp.sum(product, axis=0, keepdims=True)
    ones = jnp.ones((8, BLOCK), jnp.float32)
    total = lax.dot_general(
        ones, sums[...], (((1,), (1,)), ((), ())),
        precision=lax.Precision.HIGHEST, preferred_element_type=jnp.float32,
    )
    grads_ref[...] = total[0:1, :] * (1.0 / 512)


def finish(pos, got, ctrl_blocks):
    return pl.pallas_call(
        finish_kernel,
        out_shape=(
            jax.ShapeDtypeStruct((2, 16, NB * BLOCK), jnp.float32),
            jax.ShapeDtypeStruct((1, CONTROLS), jnp.float32),
        ),
        in_specs=[smem(), vmem(), vmem()],
        out_specs=(vmem(), vmem()),
        scratch_shapes=[
            pltpu.VMEM((SLOTS * 64, BLOCK), jnp.float32),
            pltpu.VMEM((NB, 64, BLOCK), BF),
            pltpu.VMEM((NB, 64, BLOCK), jnp.float32),
            pltpu.VMEM((CONTROLS, BLOCK), jnp.float32),
        ],
        compiler_params=pltpu.CompilerParams(vmem_limit_bytes=8 << 20),
        name="finish",
    )(pos, got, ctrl_blocks)


def shared(values, axes, count):
    spread = jnp.broadcast_to(values[None], (count,) + values.shape)
    return lax.all_to_all(spread, axes, 0, 0)


def shards(drift, ctrl_blocks, blk_pos, amps, init_states, targets):
    pieces, begin = prepare(ctrl_blocks, init_states, targets)
    over_z = shared(source(drift, amps), ("zl", "zh"), ZL * ZH)
    over_z = over_z.reshape(ZL, ZH, KEPT, 4, BLOCK).transpose(0, 2, 1, 3, 4)
    own = shared(over_z.reshape(ZL * KEPT, ZH * 4, BLOCK), ("x", "y"), X * Y)
    other = lax.ppermute(own, "c", [(0, 1), (1, 0)])
    sent = own.reshape(X, Y, ZL, KEPT, 16, BLOCK)[:, 0, :, KEPT - 1, 0:3]
    sent = jnp.sum(sent.astype(jnp.float32), axis=2).transpose(1, 0, 2).reshape(SLOTS, BLOCK)
    free = 1 - kept_half(jnp.arange(SLOTS)[:, None], lax.axis_index("c"))
    amps_all = jnp.where(free == 0, sent[:, 0:CONTROLS], sent[:, HALF : HALF + CONTROLS])

    rows = jnp.concatenate([blk_pos[:, 0], blk_pos[:, 1]])
    cols = jnp.concatenate([blk_pos[:, 1], blk_pos[:, 0]])
    number = jnp.arange(2 * CONTROLS)
    key = (rows * NB + cols) * (2 * CONTROLS) + number
    rank = jnp.sum(key[None, :] < key[:, None], axis=1)
    chosen = rank[None, :] == number[:, None]
    key = jnp.sum(jnp.where(chosen, key[None, :], 0), axis=1)
    place = key // (2 * CONTROLS)
    again = jnp.concatenate([jnp.zeros((1,), bool), place[1:] == place[:-1]])
    meta = jnp.stack([place // NB * BLOCK, place % NB * BLOCK, key % (2 * CONTROLS), again])
    meta = meta.astype(jnp.int32)

    out = chain(amps_all, meta, own, other, pieces, begin)
    got = lax.all_to_all(out, ("zl", "x"), 0, 0)
    states, partial_grads = finish(blk_pos, got, ctrl_blocks)
    grads = jnp.sum(shared(partial_grads, ("y", "zh", "c"), Y * ZH * CORES), axis=0)
    return states[None], grads


def solution(mesh):
    split = jax.sharding.Mesh(
        mesh.devices.reshape(ZL, X, Y, ZH, CORES), ("zl", "x", "y", "zh", "c")
    )
    slot, row = ("zl", "x"), ("y", "zh", "c")
    in_specs = (
        P(slot + row, None),
        P(),
        P(),
        P(slot, None),
        P(None, row, None),
        P(None, row, None),
    )
    out_specs = (P(slot, None, row, None), P(slot, None))
    return jax.shard_map(shards, mesh=split, in_specs=in_specs, out_specs=out_specs, check_vma=False)
```

```python
import functools

import jax
import jax.numpy as jnp
from jax import lax
from jax.experimental import pallas as pl
from jax.experimental.pallas import tpu as pltpu
from jax.sharding import PartitionSpec as P

ZL, X, Y, ZH, CORES = 4, 4, 4, 4, 2
BLOCK = 128
NB = 16
KEPT = NB // 2 + 1
HALF = BLOCK // 2
BAND = 64
SLOTS = 16
CONTROLS = 16
BF = jnp.bfloat16


def source_of(index):
    r = index & 3
    zh = (index >> 2) & 3
    y = (index >> 4) & 3
    c = index >> 6
    return y * 32 + zh * 8 + c * 4 + r


def pick_matrix(dtype):
    rows = lax.broadcasted_iota(jnp.int32, (BLOCK, BLOCK), 0)
    cols = lax.broadcasted_iota(jnp.int32, (BLOCK, BLOCK), 1)
    return jnp.where(source_of(rows) == cols, 1.0, 0.0).astype(dtype)


def mm(a, b):
    return jnp.dot(a, b, preferred_element_type=jnp.float32)


def mm_t(a, b):
    return lax.dot_general(a, b, (((1,), (1,)), ((), ())), preferred_element_type=jnp.float32)


def at(start, size=BLOCK):
    return pl.ds(pl.multiple_of(start, size), size)


def this_member():
    return lax.axis_index("zl") * X + lax.axis_index("x")


def kept_half(member, core):
    return jnp.where(member < SLOTS // 2, core, 1 - core)


def source_kernel(drift_ref, amps_ref, packet_ref):
    member = this_member()
    pick = pick_matrix(BF)
    for step in range(KEPT - 1):
        block = lax.rem(member + step, NB)
        packet_ref[step] = mm_t(drift_ref[:, at(block * BLOCK)], pick).astype(BF)
    block = lax.rem(member + KEPT - 1, NB)
    kept = mm_t(drift_ref[:, at(block * BLOCK)], pick)
    lane = lax.broadcasted_iota(jnp.int32, (4, BLOCK), 1)
    amps = amps_ref[...]
    high = amps.astype(BF).astype(jnp.float32)
    middle = (amps - high).astype(BF).astype(jnp.float32)
    low = amps - high - middle
    part = lax.broadcasted_iota(jnp.int32, (4, CONTROLS), 0)
    parts = jnp.where(part == 0, high, jnp.where(part == 1, middle, jnp.where(part == 2, low, 0.0)))
    number = lax.broadcasted_iota(jnp.int32, (CONTROLS, BLOCK), 0)
    column = lax.broadcasted_iota(jnp.int32, (CONTROLS, BLOCK), 1)
    spread = jnp.where((column & (HALF - 1)) == number, 1.0, 0.0).astype(BF)
    parts = mm(parts.astype(BF), spread)
    mine = (lane >= HALF) == (kept_half(member, lax.axis_index("c")) == 1)
    packet_ref[KEPT - 1] = jnp.where(mine, kept, parts).astype(BF)


def prepare_kernel(ctrl_ref, init_ref, target_ref, pieces_ref, begin_ref):
    member = this_member()
    backward = member >= SLOTS // 2
    lane = lax.rem(member, SLOTS // 2)
    pick = pick_matrix(BF)
    for k in range(CONTROLS):
        turned = mm(pick, ctrl_ref[k]).astype(BF)
        pieces_ref[k] = mm_t(turned, pick).astype(BF)
        pieces_ref[CONTROLS + k] = mm_t(pick, turned).astype(BF)

    begin_ref[...] = jnp.zeros_like(begin_ref)

    def load_from(ref):
        for part in range(2):
            for half in range(2):
                row = part * 4 + half
                begin_ref[row : row + 1, :] = ref[part, pl.ds(lane + half * 8, 1), :]

    @pl.when(backward)
    def _():
        load_from(target_ref)

    @pl.when(jnp.logical_not(backward))
    def _():
        load_from(init_ref)

    for block in range(NB):
        cols = slice(block * BLOCK, (block + 1) * BLOCK)
        value = begin_ref[:, cols]
        high = value.astype(BF)
        rest = value - high.astype(jnp.float32)
        middle = rest.astype(BF)
        low = (rest - middle.astype(jnp.float32)).astype(BF)
        begin_ref[:, cols] = mm_t(high, pick) + mm_t(middle, pick) + mm_t(low, pick)


def chain_kernel(
    amps_ref, meta_ref, own_ref, sent_ref, pieces_ref, begin_ref, out_ref,
    even_h, odd_h, x_ref, base_ref, other_ref, sems,
):
    core = lax.axis_index("c")
    backward = this_member() >= SLOTS // 2

    def piece(block_row, step):
        zl_of = lax.div(block_row, X)
        x_of = lax.rem(block_row, X)
        mine, theirs = (
            jnp.concatenate([ref[x_of * Y + y, zl_of * KEPT + step] for y in range(Y)], axis=0)
            for ref in (own_ref, other_ref)
        )
        first = jnp.where(core == 0, mine, theirs)
        second = jnp.where(core == 0, theirs, mine)
        return jnp.concatenate([first, second], axis=0)

    def put(row, col, block):
        for ham in (even_h, odd_h):
            ham[at(row * BLOCK), at(col * BLOCK)] = block

    def lay(block_row):
        put(block_row, block_row, piece(block_row, 0))
        for step in range(1, KEPT - 1):
            col = lax.rem(block_row + step, NB)
            block = piece(block_row, step)
            put(block_row, col, block)
            put(col, block_row, block.T)

    def fetch(x_of):
        part = pl.ds(x_of * Y, Y)
        return pltpu.make_async_copy(sent_ref.at[part], other_ref.at[part], sems.at[x_of])

    for x_of in range(X):
        fetch(x_of).start()
    for x_of in range(X):
        fetch(x_of).wait()

        def lay_next(zl_of, _, x_of=x_of):
            lay(zl_of * X + x_of)
            return 0

        lax.fori_loop(0, ZL, lay_next, 0)

    low_row = lax.broadcasted_iota(jnp.int32, (BLOCK, BLOCK), 0) < HALF
    low_col = lax.broadcasted_iota(jnp.int32, (BLOCK, BLOCK), 1) < HALF
    diagonal = jnp.where(low_row == low_col, 1.0, 0.0).astype(BF)
    crossed = jnp.where(low_row == low_col, 0.0, 1.0).astype(BF)

    def lay_shared(block_row, _):
        col = block_row + NB // 2
        upper, lower = piece(block_row, KEPT - 1), piece(col, KEPT - 1)
        put(block_row, col, upper * diagonal + lower.T * crossed)
        put(col, block_row, upper.T * diagonal + lower * crossed)
        return 0

    lax.fori_loop(0, NB // 2, lay_shared, 0, unroll=2)

    def gather_base(p, _):
        base_ref[p] = even_h[at(meta_ref[0, p]), at(meta_ref[1, p])]
        return 0

    lax.fori_loop(0, 2 * CONTROLS, gather_base, 0)

    def slot_of(step):
        return jnp.where(backward, SLOTS - 1 - step, step)

    def tasks(step, target):
        slot = slot_of(jnp.minimum(step, SLOTS - 1))
        total = [None]

        def task(q):
            band, p = divmod(q, 2 * CONTROLS)
            part = slice(band * BAND, (band + 1) * BAND)
            which = meta_ref[2, p]
            start = base_ref[p, part].astype(jnp.float32)
            if p > 0:
                start = jnp.where(meta_ref[3, p] == 0, start, total[0])
            amp = amps_ref[slot, lax.rem(which, CONTROLS)]
            total[0] = start + amp * pieces_ref[which, part].astype(jnp.float32)
            rows = pl.ds(pl.multiple_of(meta_ref[0, p] + band * BAND, BAND), BAND)
            target[rows, at(meta_ref[1, p])] = total[0].astype(BF)

        return [functools.partial(task, q) for q in range(2 * CONTROLS * BLOCK // BAND)]

    x_ref[...] = begin_ref[...]

    def write(place):
        for quad in range(NB // 4):
            halves = []
            for pair in (2 * quad, 2 * quad + 1):
                first = x_ref[:, 2 * pair * BLOCK : (2 * pair + 1) * BLOCK]
                second = x_ref[:, (2 * pair + 1) * BLOCK : (2 * pair + 2) * BLOCK]
                halves.append(first + pltpu.roll(second, 2, axis=0))
            out_ref[place, quad * 16 : (quad + 1) * 16, :] = jnp.concatenate(halves, axis=0).astype(BF)

    @pl.when(backward)
    def _():
        write(SLOTS - 1)

    row_of = lax.broadcasted_iota(jnp.int32, (8, BLOCK), 0)
    sign = jnp.where((row_of < 4) == jnp.logical_not(backward), 1.0, -1.0)
    sign = jnp.concatenate([sign] * NB, axis=1)

    def applied(values, ham, todo):
        rounded = values.astype(BF)
        found = []
        for n in range(NB // 2):
            found.append(mm(rounded, ham[:, n * 256 : (n + 1) * 256]))
            for task in todo[2 * n : 2 * n + 2]:
                task()
        return jnp.concatenate(found, axis=1)

    def advance(step, ham, following):
        todo = tasks(step + 1, following)
        start = x_ref[...]
        u1 = applied(start, ham, todo[0:16])
        x_ref[...] = sign * pltpu.roll(u1, 4, axis=0) + start
        u2 = applied(u1, ham, todo[16:32]) * (1.0 / 2)
        u3 = applied(u2, ham, todo[32:48]) * (1.0 / 3)
        x_ref[...] = x_ref[...] - u2 - sign * pltpu.roll(u3, 4, axis=0)
        u4 = applied(u3, ham, todo[48:64]) * (1.0 / 4)
        x_ref[...] = x_ref[...] + u4
        place = jnp.where(backward, SLOTS - 2 - step, step)

        @pl.when(place >= 0)
        def _():
            write(place)

    for task in tasks(0, even_h):
        task()

    def two_slots(pair, _):
        advance(2 * pair, even_h, odd_h)
        advance(2 * pair + 1, odd_h, even_h)
        return 0

    lax.fori_loop(0, SLOTS // 2, two_slots, 0)


def vmem():
    return pl.BlockSpec(memory_space=pltpu.VMEM)


def smem():
    return pl.BlockSpec(memory_space=pltpu.SMEM)


def source(drift, amps):
    return pl.pallas_call(
        source_kernel,
        out_shape=jax.ShapeDtypeStruct((KEPT, 4, BLOCK), BF),
        in_specs=[vmem(), vmem()],
        out_specs=vmem(),
        compiler_params=pltpu.CompilerParams(vmem_limit_bytes=2 << 20),
        name="source",
    )(drift, amps)


def prepare(ctrl_blocks, init_states, targets):
    return pl.pallas_call(
        prepare_kernel,
        out_shape=(
            jax.ShapeDtypeStruct((2 * CONTROLS, BLOCK, BLOCK), BF),
            jax.ShapeDtypeStruct((8, NB * BLOCK), jnp.float32),
        ),
        in_specs=[vmem()] * 3,
        out_specs=(vmem(), vmem()),
        compiler_params=pltpu.CompilerParams(vmem_limit_bytes=6 << 20),
        cost_estimate=pl.CostEstimate(
            flops=2 * 3 * CONTROLS * BLOCK**3, bytes_accessed=8 << 20, transcendentals=0
        ),
        name="prepare",
    )(ctrl_blocks, init_states, targets)


def chain(amps, meta, own, other, pieces, begin):
    extent = NB * BLOCK
    return pl.pallas_call(
        chain_kernel,
        out_shape=jax.ShapeDtypeStruct((SLOTS, 64, BLOCK), BF),
        in_specs=[smem(), smem(), vmem(), pl.BlockSpec(memory_space=pl.ANY), vmem(), vmem()],
        out_specs=vmem(),
        scratch_shapes=[
            pltpu.VMEM((extent, extent), BF),
            pltpu.VMEM((extent, extent), BF),
            pltpu.VMEM((8, extent), jnp.float32),
            pltpu.VMEM((2 * CONTROLS, BLOCK, BLOCK), BF),
            pltpu.VMEM((X * Y, ZL * KEPT, 16, BLOCK), BF),
            pltpu.SemaphoreType.DMA((X,)),
        ],
        compiler_params=pltpu.CompilerParams(vmem_limit_bytes=30 << 20),
        cost_estimate=pl.CostEstimate(
            flops=2 * 8 * 64 * extent**2, bytes_accessed=8 << 20, transcendentals=0
        ),
        name="chain",
    )(amps, meta, own, other, pieces, begin)


def finish_kernel(pos_ref, got_ref, ctrl_ref, states_ref, grads_ref, flat, left, right, sums):
    pick = pick_matrix(BF)
    for member in range(SLOTS):
        flat[member * 64 : (member + 1) * 64, :] = mm(got_ref[member], pick)
    for block in range(NB):
        pair, side = block // 2, block % 2
        cols = slice(block * BLOCK, (block + 1) * BLOCK)
        found = {}
        for which in range(2):
            for part in range(2):
                halves = []
                for half in range(2):
                    start = which * 512 + pair * 8 + part * 4 + side * 2 + half
                    value = flat[pl.ds(start, 8, stride=64), :]
                    if which == 0:
                        states_ref[part, half * 8 : (half + 1) * 8, cols] = value
                    halves.append(value)
                found[which, part] = jnp.concatenate(halves, axis=0)
        weights = [found[1, 0], found[1, 1]]
        source = [found[0, 1], -found[0, 0]]
        left[block] = jnp.concatenate(weights + source, axis=0).astype(BF)
        right[block] = jnp.concatenate(source + weights, axis=0)
    for k in range(CONTROLS):
        product = mm(left[pos_ref[k, 0]], ctrl_ref[k]) * right[pos_ref[k, 1]]
        sums[k : k + 1, :] = jnp.sum(product, axis=0, keepdims=True)
    ones = jnp.ones((8, BLOCK), jnp.float32)
    total = lax.dot_general(
        ones, sums[...], (((1,), (1,)), ((), ())),
        precision=lax.Precision.HIGHEST, preferred_element_type=jnp.float32,
    )
    grads_ref[...] = total[0:1, :] * (1.0 / 512)


def finish(pos, got, ctrl_blocks):
    return pl.pallas_call(
        finish_kernel,
        out_shape=(
            jax.ShapeDtypeStruct((2, 16, NB * BLOCK), jnp.float32),
            jax.ShapeDtypeStruct((1, CONTROLS), jnp.float32),
        ),
        in_specs=[smem(), vmem(), vmem()],
        out_specs=(vmem(), vmem()),
        scratch_shapes=[
            pltpu.VMEM((SLOTS * 64, BLOCK), jnp.float32),
            pltpu.VMEM((NB, 64, BLOCK), BF),
            pltpu.VMEM((NB, 64, BLOCK), jnp.float32),
            pltpu.VMEM((CONTROLS, BLOCK), jnp.float32),
        ],
        compiler_params=pltpu.CompilerParams(vmem_limit_bytes=8 << 20),
        name="finish",
    )(pos, got, ctrl_blocks)


def shared(values, axes, count):
    spread = jnp.broadcast_to(values[None], (count,) + values.shape)
    return lax.all_to_all(spread, axes, 0, 0)


def shards(drift, ctrl_blocks, blk_pos, amps, init_states, targets):
    pieces, begin = prepare(ctrl_blocks, init_states, targets)
    over_z = shared(source(drift, amps), ("zl", "zh"), ZL * ZH)
    over_z = over_z.reshape(ZL, ZH, KEPT, 4, BLOCK).transpose(0, 2, 1, 3, 4)
    own = shared(over_z.reshape(ZL * KEPT, ZH * 4, BLOCK), ("x", "y"), X * Y)
    other = lax.ppermute(own, "c", [(0, 1), (1, 0)])
    sent = own.reshape(X, Y, ZL, KEPT, 16, BLOCK)[:, 0, :, KEPT - 1, 0:3]
    sent = jnp.sum(sent.astype(jnp.float32), axis=2).transpose(1, 0, 2).reshape(SLOTS, BLOCK)
    free = 1 - kept_half(jnp.arange(SLOTS)[:, None], lax.axis_index("c"))
    amps_all = jnp.where(free == 0, sent[:, 0:CONTROLS], sent[:, HALF : HALF + CONTROLS])

    rows = jnp.concatenate([blk_pos[:, 0], blk_pos[:, 1]])
    cols = jnp.concatenate([blk_pos[:, 1], blk_pos[:, 0]])
    number = jnp.arange(2 * CONTROLS)
    key = (rows * NB + cols) * (2 * CONTROLS) + number
    rank = jnp.sum(key[None, :] < key[:, None], axis=1)
    chosen = rank[None, :] == number[:, None]
    key = jnp.sum(jnp.where(chosen, key[None, :], 0), axis=1)
    place = key // (2 * CONTROLS)
    again = jnp.concatenate([jnp.zeros((1,), bool), place[1:] == place[:-1]])
    meta = jnp.stack([place // NB * BLOCK, place % NB * BLOCK, key % (2 * CONTROLS), again])
    meta = meta.astype(jnp.int32)

    out = chain(amps_all, meta, own, other, pieces, begin)
    got = lax.all_to_all(out, ("zl", "x"), 0, 0)
    states, partial_grads = finish(blk_pos, got, ctrl_blocks)
    grads = jnp.sum(shared(partial_grads, ("y", "zh", "c"), Y * ZH * CORES), axis=0)
    return states[None], grads


def solution(mesh):
    split = jax.sharding.Mesh(
        mesh.devices.reshape(ZL, X, Y, ZH, CORES), ("zl", "x", "y", "zh", "c")
    )
    slot, row = ("zl", "x"), ("y", "zh", "c")
    in_specs = (
        P(slot + row, None),
        P(),
        P(),
        P(slot, None),
        P(None, row, None),
        P(None, row, None),
    )
    out_specs = (P(slot, None, row, None), P(slot, None))
    return jax.shard_map(shards, mesh=split, in_specs=in_specs, out_specs=out_specs, check_vma=False)
```

```python
import functools

import jax
import jax.numpy as jnp
from jax import lax
from jax.experimental import pallas as pl
from jax.experimental.pallas import tpu as pltpu
from jax.sharding import PartitionSpec as P

ZL, X, Y, ZH, CORES = 4, 4, 4, 4, 2
BLOCK = 128
NB = 16
KEPT = NB // 2 + 1
HALF = BLOCK // 2
BAND = 64
SLOTS = 16
CONTROLS = 16
BF = jnp.bfloat16


def source_of(index):
    r = index & 3
    zh = (index >> 2) & 3
    y = (index >> 4) & 3
    c = index >> 6
    return y * 32 + zh * 8 + c * 4 + r


def pick_matrix(dtype):
    rows = lax.broadcasted_iota(jnp.int32, (BLOCK, BLOCK), 0)
    cols = lax.broadcasted_iota(jnp.int32, (BLOCK, BLOCK), 1)
    return jnp.where(source_of(rows) == cols, 1.0, 0.0).astype(dtype)


def mm(a, b):
    return jnp.dot(a, b, preferred_element_type=jnp.float32)


def mm_t(a, b):
    return lax.dot_general(a, b, (((1,), (1,)), ((), ())), preferred_element_type=jnp.float32)


def at(start, size=BLOCK):
    return pl.ds(pl.multiple_of(start, size), size)


def this_member():
    return lax.axis_index("zl") * X + lax.axis_index("x")


def kept_half(member, core):
    return jnp.where(member < SLOTS // 2, core, 1 - core)


def source_kernel(drift_ref, amps_ref, packet_ref):
    member = this_member()
    pick = pick_matrix(BF)
    for step in range(KEPT - 1):
        block = lax.rem(member + step, NB)
        packet_ref[step] = mm_t(drift_ref[:, at(block * BLOCK)], pick).astype(BF)
    block = lax.rem(member + KEPT - 1, NB)
    kept = mm_t(drift_ref[:, at(block * BLOCK)], pick)
    lane = lax.broadcasted_iota(jnp.int32, (4, BLOCK), 1)
    amps = amps_ref[...]
    high = amps.astype(BF).astype(jnp.float32)
    middle = (amps - high).astype(BF).astype(jnp.float32)
    low = amps - high - middle
    part = lax.broadcasted_iota(jnp.int32, (4, CONTROLS), 0)
    parts = jnp.where(part == 0, high, jnp.where(part == 1, middle, jnp.where(part == 2, low, 0.0)))
    number = lax.broadcasted_iota(jnp.int32, (CONTROLS, BLOCK), 0)
    column = lax.broadcasted_iota(jnp.int32, (CONTROLS, BLOCK), 1)
    spread = jnp.where((column & (HALF - 1)) == number, 1.0, 0.0).astype(BF)
    parts = mm(parts.astype(BF), spread)
    mine = (lane >= HALF) == (kept_half(member, lax.axis_index("c")) == 1)
    packet_ref[KEPT - 1] = jnp.where(mine, kept, parts).astype(BF)


def prepare_kernel(ctrl_ref, init_ref, target_ref, pieces_ref, begin_ref):
    member = this_member()
    backward = member >= SLOTS // 2
    lane = lax.rem(member, SLOTS // 2)
    pick = pick_matrix(BF)
    for k in range(CONTROLS):
        turned = mm(pick, ctrl_ref[k]).astype(BF)
        pieces_ref[k] = mm_t(turned, pick).astype(BF)
        pieces_ref[CONTROLS + k] = mm_t(pick, turned).astype(BF)

    begin_ref[...] = jnp.zeros_like(begin_ref)

    def load_from(ref):
        for part in range(2):
            for half in range(2):
                row = part * 4 + half
                begin_ref[row : row + 1, :] = ref[part, pl.ds(lane + half * 8, 1), :]

    @pl.when(backward)
    def _():
        load_from(target_ref)

    @pl.when(jnp.logical_not(backward))
    def _():
        load_from(init_ref)

    for block in range(NB):
        cols = slice(block * BLOCK, (block + 1) * BLOCK)
        value = begin_ref[:, cols]
        high = value.astype(BF)
        rest = value - high.astype(jnp.float32)
        middle = rest.astype(BF)
        low = (rest - middle.astype(jnp.float32)).astype(BF)
        begin_ref[:, cols] = mm_t(high, pick) + mm_t(middle, pick) + mm_t(low, pick)


def chain_kernel(
    amps_ref, meta_ref, own_ref, sent_ref, pieces_ref, begin_ref, out_ref,
    even_h, odd_h, x_ref, base_ref, other_ref, sems,
):
    core = lax.axis_index("c")
    backward = this_member() >= SLOTS // 2

    def piece(block_row, step):
        zl_of = lax.div(block_row, X)
        x_of = lax.rem(block_row, X)
        mine, theirs = (
            jnp.concatenate([ref[x_of * Y + y, zl_of * KEPT + step] for y in range(Y)], axis=0)
            for ref in (own_ref, other_ref)
        )
        first = jnp.where(core == 0, mine, theirs)
        second = jnp.where(core == 0, theirs, mine)
        return jnp.concatenate([first, second], axis=0)

    def put(row, col, block):
        for ham in (even_h, odd_h):
            ham[at(row * BLOCK), at(col * BLOCK)] = block

    def lay(block_row):
        put(block_row, block_row, piece(block_row, 0))
        for step in range(1, KEPT - 1):
            col = lax.rem(block_row + step, NB)
            block = piece(block_row, step)
            put(block_row, col, block)
            put(col, block_row, block.T)

    def fetch(x_of):
        part = pl.ds(x_of * Y, Y)
        return pltpu.make_async_copy(sent_ref.at[part], other_ref.at[part], sems.at[x_of])

    for x_of in range(X):
        fetch(x_of).start()
    for x_of in range(X):
        fetch(x_of).wait()

        def lay_next(zl_of, _, x_of=x_of):
            lay(zl_of * X + x_of)
            return 0

        lax.fori_loop(0, ZL, lay_next, 0, unroll=2)

    low_row = lax.broadcasted_iota(jnp.int32, (BLOCK, BLOCK), 0) < HALF
    low_col = lax.broadcasted_iota(jnp.int32, (BLOCK, BLOCK), 1) < HALF
    diagonal = jnp.where(low_row == low_col, 1.0, 0.0).astype(BF)
    crossed = jnp.where(low_row == low_col, 0.0, 1.0).astype(BF)

    def lay_shared(block_row, _):
        col = block_row + NB // 2
        upper, lower = piece(block_row, KEPT - 1), piece(col, KEPT - 1)
        put(block_row, col, upper * diagonal + lower.T * crossed)
        put(col, block_row, upper.T * diagonal + lower * crossed)
        return 0

    lax.fori_loop(0, NB // 2, lay_shared, 0, unroll=2)

    def gather_base(p, _):
        base_ref[p] = even_h[at(meta_ref[0, p]), at(meta_ref[1, p])]
        return 0

    lax.fori_loop(0, 2 * CONTROLS, gather_base, 0)

    def slot_of(step):
        return jnp.where(backward, SLOTS - 1 - step, step)

    def tasks(step, target):
        slot = slot_of(jnp.minimum(step, SLOTS - 1))
        total = [None]

        def task(q):
            band, p = divmod(q, 2 * CONTROLS)
            part = slice(band * BAND, (band + 1) * BAND)
            which = meta_ref[2, p]
            start = base_ref[p, part].astype(jnp.float32)
            if p > 0:
                start = jnp.where(meta_ref[3, p] == 0, start, total[0])
            amp = amps_ref[slot, lax.rem(which, CONTROLS)]
            total[0] = start + amp * pieces_ref[which, part].astype(jnp.float32)
            rows = pl.ds(pl.multiple_of(meta_ref[0, p] + band * BAND, BAND), BAND)
            target[rows, at(meta_ref[1, p])] = total[0].astype(BF)

        return [functools.partial(task, q) for q in range(2 * CONTROLS * BLOCK // BAND)]

    x_ref[...] = begin_ref[...]

    def write(place):
        for quad in range(NB // 4):
            halves = []
            for pair in (2 * quad, 2 * quad + 1):
                first = x_ref[:, 2 * pair * BLOCK : (2 * pair + 1) * BLOCK]
                second = x_ref[:, (2 * pair + 1) * BLOCK : (2 * pair + 2) * BLOCK]
                halves.append(first + pltpu.roll(second, 2, axis=0))
            out_ref[place, quad * 16 : (quad + 1) * 16, :] = jnp.concatenate(halves, axis=0).astype(BF)

    @pl.when(backward)
    def _():
        write(SLOTS - 1)

    row_of = lax.broadcasted_iota(jnp.int32, (8, BLOCK), 0)
    sign = jnp.where((row_of < 4) == jnp.logical_not(backward), 1.0, -1.0)
    sign = jnp.concatenate([sign] * NB, axis=1)

    def applied(values, ham, todo):
        rounded = values.astype(BF)
        found = []
        for n in range(NB // 2):
            found.append(mm(rounded, ham[:, n * 256 : (n + 1) * 256]))
            for task in todo[2 * n : 2 * n + 2]:
                task()
        return jnp.concatenate(found, axis=1)

    def advance(step, ham, following):
        todo = tasks(step + 1, following)
        start = x_ref[...]
        u1 = applied(start, ham, todo[0:16])
        x_ref[...] = sign * pltpu.roll(u1, 4, axis=0) + start
        u2 = applied(u1, ham, todo[16:32]) * (1.0 / 2)
        u3 = applied(u2, ham, todo[32:48]) * (1.0 / 3)
        x_ref[...] = x_ref[...] - u2 - sign * pltpu.roll(u3, 4, axis=0)
        u4 = applied(u3, ham, todo[48:64]) * (1.0 / 4)
        x_ref[...] = x_ref[...] + u4
        place = jnp.where(backward, SLOTS - 2 - step, step)

        @pl.when(place >= 0)
        def _():
            write(place)

    for task in tasks(0, even_h):
        task()

    def two_slots(pair, _):
        advance(2 * pair, even_h, odd_h)
        advance(2 * pair + 1, odd_h, even_h)
        return 0

    lax.fori_loop(0, SLOTS // 2, two_slots, 0)


def vmem():
    return pl.BlockSpec(memory_space=pltpu.VMEM)


def smem():
    return pl.BlockSpec(memory_space=pltpu.SMEM)


def source(drift, amps):
    return pl.pallas_call(
        source_kernel,
        out_shape=jax.ShapeDtypeStruct((KEPT, 4, BLOCK), BF),
        in_specs=[vmem(), vmem()],
        out_specs=vmem(),
        compiler_params=pltpu.CompilerParams(vmem_limit_bytes=2 << 20),
        name="source",
    )(drift, amps)


def prepare(ctrl_blocks, init_states, targets):
    return pl.pallas_call(
        prepare_kernel,
        out_shape=(
            jax.ShapeDtypeStruct((2 * CONTROLS, BLOCK, BLOCK), BF),
            jax.ShapeDtypeStruct((8, NB * BLOCK), jnp.float32),
        ),
        in_specs=[vmem()] * 3,
        out_specs=(vmem(), vmem()),
        compiler_params=pltpu.CompilerParams(vmem_limit_bytes=6 << 20),
        cost_estimate=pl.CostEstimate(
            flops=2 * 3 * CONTROLS * BLOCK**3, bytes_accessed=8 << 20, transcendentals=0
        ),
        name="prepare",
    )(ctrl_blocks, init_states, targets)


def chain(amps, meta, own, other, pieces, begin):
    extent = NB * BLOCK
    return pl.pallas_call(
        chain_kernel,
        out_shape=jax.ShapeDtypeStruct((SLOTS, 64, BLOCK), BF),
        in_specs=[smem(), smem(), vmem(), pl.BlockSpec(memory_space=pl.ANY), vmem(), vmem()],
        out_specs=vmem(),
        scratch_shapes=[
            pltpu.VMEM((extent, extent), BF),
            pltpu.VMEM((extent, extent), BF),
            pltpu.VMEM((8, extent), jnp.float32),
            pltpu.VMEM((2 * CONTROLS, BLOCK, BLOCK), BF),
            pltpu.VMEM((X * Y, ZL * KEPT, 16, BLOCK), BF),
            pltpu.SemaphoreType.DMA((X,)),
        ],
        compiler_params=pltpu.CompilerParams(vmem_limit_bytes=30 << 20),
        cost_estimate=pl.CostEstimate(
            flops=2 * 8 * 64 * extent**2, bytes_accessed=8 << 20, transcendentals=0
        ),
        name="chain",
    )(amps, meta, own, other, pieces, begin)


def finish_kernel(pos_ref, got_ref, ctrl_ref, states_ref, grads_ref, flat, left, right, sums):
    pick = pick_matrix(BF)
    for member in range(SLOTS):
        flat[member * 64 : (member + 1) * 64, :] = mm(got_ref[member], pick)
    for block in range(NB):
        pair, side = block // 2, block % 2
        cols = slice(block * BLOCK, (block + 1) * BLOCK)
        found = {}
        for which in range(2):
            for part in range(2):
                halves = []
                for half in range(2):
                    start = which * 512 + pair * 8 + part * 4 + side * 2 + half
                    value = flat[pl.ds(start, 8, stride=64), :]
                    if which == 0:
                        states_ref[part, half * 8 : (half + 1) * 8, cols] = value
                    halves.append(value)
                found[which, part] = jnp.concatenate(halves, axis=0)
        weights = [found[1, 0], found[1, 1]]
        source = [found[0, 1], -found[0, 0]]
        left[block] = jnp.concatenate(weights + source, axis=0).astype(BF)
        right[block] = jnp.concatenate(source + weights, axis=0)
    for k in range(CONTROLS):
        product = mm(left[pos_ref[k, 0]], ctrl_ref[k]) * right[pos_ref[k, 1]]
        sums[k : k + 1, :] = jnp.sum(product, axis=0, keepdims=True)
    ones = jnp.ones((8, BLOCK), jnp.float32)
    total = lax.dot_general(
        ones, sums[...], (((1,), (1,)), ((), ())),
        precision=lax.Precision.HIGHEST, preferred_element_type=jnp.float32,
    )
    grads_ref[...] = total[0:1, :] * (1.0 / 512)


def finish(pos, got, ctrl_blocks):
    return pl.pallas_call(
        finish_kernel,
        out_shape=(
            jax.ShapeDtypeStruct((2, 16, NB * BLOCK), jnp.float32),
            jax.ShapeDtypeStruct((1, CONTROLS), jnp.float32),
        ),
        in_specs=[smem(), vmem(), vmem()],
        out_specs=(vmem(), vmem()),
        scratch_shapes=[
            pltpu.VMEM((SLOTS * 64, BLOCK), jnp.float32),
            pltpu.VMEM((NB, 64, BLOCK), BF),
            pltpu.VMEM((NB, 64, BLOCK), jnp.float32),
            pltpu.VMEM((CONTROLS, BLOCK), jnp.float32),
        ],
        compiler_params=pltpu.CompilerParams(vmem_limit_bytes=8 << 20),
        name="finish",
    )(pos, got, ctrl_blocks)


def shared(values, axes, count):
    spread = jnp.broadcast_to(values[None], (count,) + values.shape)
    return lax.all_to_all(spread, axes, 0, 0)


def shards(drift, ctrl_blocks, blk_pos, amps, init_states, targets):
    pieces, begin = prepare(ctrl_blocks, init_states, targets)
    over_z = shared(source(drift, amps), ("zl", "zh"), ZL * ZH)
    over_z = over_z.reshape(ZL, ZH, KEPT, 4, BLOCK).transpose(0, 2, 1, 3, 4)
    own = shared(over_z.reshape(ZL * KEPT, ZH * 4, BLOCK), ("x", "y"), X * Y)
    other = lax.ppermute(own, "c", [(0, 1), (1, 0)])
    sent = own.reshape(X, Y, ZL, KEPT, 16, BLOCK)[:, 0, :, KEPT - 1, 0:3]
    sent = jnp.sum(sent.astype(jnp.float32), axis=2).transpose(1, 0, 2).reshape(SLOTS, BLOCK)
    free = 1 - kept_half(jnp.arange(SLOTS)[:, None], lax.axis_index("c"))
    amps_all = jnp.where(free == 0, sent[:, 0:CONTROLS], sent[:, HALF : HALF + CONTROLS])

    rows = jnp.concatenate([blk_pos[:, 0], blk_pos[:, 1]])
    cols = jnp.concatenate([blk_pos[:, 1], blk_pos[:, 0]])
    number = jnp.arange(2 * CONTROLS)
    key = (rows * NB + cols) * (2 * CONTROLS) + number
    rank = jnp.sum(key[None, :] < key[:, None], axis=1)
    chosen = rank[None, :] == number[:, None]
    key = jnp.sum(jnp.where(chosen, key[None, :], 0), axis=1)
    place = key // (2 * CONTROLS)
    again = jnp.concatenate([jnp.zeros((1,), bool), place[1:] == place[:-1]])
    meta = jnp.stack([place // NB * BLOCK, place % NB * BLOCK, key % (2 * CONTROLS), again])
    meta = meta.astype(jnp.int32)

    out = chain(amps_all, meta, own, other, pieces, begin)
    got = lax.all_to_all(out, ("zl", "x"), 0, 0)
    states, partial_grads = finish(blk_pos, got, ctrl_blocks)
    grads = jnp.sum(shared(partial_grads, ("y", "zh", "c"), Y * ZH * CORES), axis=0)
    return states[None], grads


def solution(mesh):
    split = jax.sharding.Mesh(
        mesh.devices.reshape(ZL, X, Y, ZH, CORES), ("zl", "x", "y", "zh", "c")
    )
    slot, row = ("zl", "x"), ("y", "zh", "c")
    in_specs = (
        P(slot + row, None),
        P(),
        P(),
        P(slot, None),
        P(None, row, None),
        P(None, row, None),
    )
    out_specs = (P(slot, None, row, None), P(slot, None))
    return jax.shard_map(shards, mesh=split, in_specs=in_specs, out_specs=out_specs, check_vma=False)
```
